32 devices in a mesh: ctx: 16 (over z, y, core), tp: 2 (over x).
Axes of the slice: x: 2, y: 2, z: 4, core: 2. Of those that a mesh axis runs over, the one named last changes fastest.
Arguments:
- student_rows: bfloat16 [4096, 8192], P('ctx', 'tp'), may hold values from -3 to 3
- queries: bfloat16 [4096, 4096], P('ctx', 'tp'), may hold values from -5 to 5
- keys_values: bfloat16 [2, 4096, 512], P(None, 'ctx'), may hold values from -5 to 5
- out_weight: bfloat16 [4096, 8192], P(None, 'tp'), may hold values from -0.09375 to 0.09375
- teacher_rows: bfloat16 [6144, 8192], P('ctx', 'tp'), may hold values from -6 to 6
- span_start: int32 [4096], P('ctx'), may hold values from 0 to 6143, as said below
- span_len: int32 [4096], P('ctx'), may hold values from 1 to 4, as said below
Outputs:
- student_out: bfloat16 [4096, 8192], P('ctx', 'tp')
- teacher_grad: bfloat16 [6144, 8192], P('ctx', 'tp')
The draws below stay inside these ranges and needn't reach their ends.
Inputs may be any that keep to these rules, and one draw needn't show every extreme that they name: Student token s of shard c = s // 256 pools teacher tokens span_start[s] to span_start[s] + span_len[s] - 1, all within 8 tokens of shard c's block of teacher tokens c * 384 to (c + 1) * 384 - 1. The first student token of every shard but the first starts exactly 8 tokens before that block. `span_len`: the last student token of every shard but the last ends exactly 8 tokens after its shard's block.
All inputs are finite; a program needn't handle non-finite values.
Results may differ from the reference program's by a relative error of at most 0.012.
Values may be sent and summed in bfloat16 or wider, within the bound.
No kernel may reach another device: no remote copies, remote signals or barrier semaphores. Data moves between devices by JAX's collectives and lax.ppermute only.
A program may use at most 192 MiB of HBM per device.

```python
import math
import jax
import jax.numpy as jnp
from jax import lax

D = 8192
HEADS = 32
KVH = 4
HD = 128
S_DEV = 256
JIT = 3
LMAX = 4
HALO = 8
TOKENS = 4096
TD_DEV = 384
TEACH_TOKENS = 6144
N_CTX = 16


def draw_queries(key, part):
    drawn_key = jax.random.fold_in(key, 1)
    result = 2.5 * jax.random.truncated_normal(drawn_key, -2.0, 2.0, (TOKENS, HEADS, HD), jnp.float32)
    return result.reshape(TOKENS, HEADS * HD).astype(jnp.bfloat16)


def draw_keys_values(key, part):
    key_seed = jax.random.fold_in(key, 2)
    value_seed = jax.random.fold_in(key, 3)
    key_part = jax.random.truncated_normal(key_seed, -5.0, 5.0, (TOKENS, KVH, HD), jnp.float32)
    value_part = 2.0 * jax.random.truncated_normal(value_seed, -2.5, 2.5, (TOKENS, KVH, HD), jnp.float32)
    stacked = jnp.stack([key_part.reshape(TOKENS, KVH * HD), value_part.reshape(TOKENS, KVH * HD)])
    return stacked.astype(jnp.bfloat16)


def span_table(key):
    seeded = jax.random.fold_in(key, 517)
    first_key, second_key = jax.random.split(seeded)
    rows = jnp.arange(TOKENS, dtype=jnp.int32)
    local = rows % S_DEV
    shard = rows // S_DEV
    length = jax.random.randint(first_key, (TOKENS,), 1, LMAX + 1, dtype=jnp.int32)
    jitter = jax.random.randint(second_key, (TOKENS,), -JIT, JIT + 1, dtype=jnp.int32)
    start = shard * TD_DEV + local * TD_DEV // S_DEV + jitter
    start = jnp.where(local == 0, shard * TD_DEV - HALO, start)
    length = jnp.where(local == S_DEV - 1, LMAX, length)
    start = jnp.where(local == S_DEV - 1, (shard + 1) * TD_DEV + HALO - LMAX, start)
    start = jnp.clip(start, 0, TEACH_TOKENS - length)
    return (start.astype(jnp.int32), length.astype(jnp.int32))


def draw_span_start(key, part):
    return span_table(key)[0]


def draw_span_len(key, part):
    return span_table(key)[1]


def level_of(stream_key, dims, pieces, low, high):
    gain, own = 1.0, jax.random.fold_in(stream_key, 6)
    for axis_at, parts in pieces:
        steps = jnp.exp(jax.random.uniform(jax.random.fold_in(own, axis_at), (parts,), jnp.float32, low / len(pieces), high / len(pieces)))
        gain = gain * jnp.repeat(steps, dims[axis_at] // parts).reshape([-1 if axis == axis_at else 1 for axis in range(len(dims))])
    return gain


def noise(rng, dims, scale, bound, shards=(), kind=jnp.bfloat16):
    gain = level_of(rng, dims, shards, -0.22, 0.18) if shards else 1.0
    array = jax.random.normal(rng, dims, jnp.float32) * scale * gain
    return jnp.minimum(jnp.maximum(array, -bound), bound).astype(kind)


def setup_inputs(seed: int = 0) -> dict:
    key_of = jax.random.split(jax.random.key(seed), 8)
    return {
        "student_rows": noise(key_of[0], (TOKENS, D), 0.5, 3.0, ((0, 16), (1, 2))),
        "queries": draw_queries(jax.random.fold_in(key_of[7], 71), 0),
        "keys_values": draw_keys_values(jax.random.fold_in(key_of[7], 71), 0),
        "out_weight": noise(key_of[3], (HEADS * HD, D), (HEADS * HD) ** -0.5, 0.09375, ((1, 2),)),
        "teacher_rows": noise(key_of[4], (TEACH_TOKENS, D), 1.0, 6.0, ((0, 16), (1, 2))),
        "span_start": draw_span_start(jax.random.fold_in(key_of[7], 71), 0),
        "span_len": draw_span_len(jax.random.fold_in(key_of[7], 71), 0),
    }


def reference(student_rows, queries, keys_values, out_weight, teacher_rows, span_start, span_len):
    score_scale = 1.0 / math.sqrt(HD)
    group_size = HEADS // KVH
    block_rows = math.gcd(TOKENS, 512)
    block_count = TOKENS // block_rows
    query_cube = queries.reshape(TOKENS, HEADS, HD)

    def head_block(index):
        head_index = (index // block_count).astype(jnp.int32)
        block_index = (index % block_count).astype(jnp.int32)
        query_rows = lax.dynamic_slice(query_cube, (block_index * block_rows, head_index, jnp.int32(0)), (block_rows, 1, HD)).reshape(block_rows, HD)
        kv_col = (head_index // group_size * HD).astype(jnp.int32)
        key_rows = lax.dynamic_slice(keys_values[0], (jnp.int32(0), kv_col), (TOKENS, HD))
        value_rows = lax.dynamic_slice(keys_values[1], (jnp.int32(0), kv_col), (TOKENS, HD))
        scores = jnp.dot(query_rows, key_rows.T, preferred_element_type=jnp.float32) * score_scale
        query_pos = block_index * block_rows + jnp.arange(block_rows, dtype=jnp.int32)
        key_pos = jnp.arange(TOKENS, dtype=jnp.int32)
        visible = key_pos[None, :] <= query_pos[:, None]
        scores = jnp.where(visible, scores, jnp.float32(-1e+30))
        row_peak = lax.optimization_barrier(jnp.max(scores, axis=1, keepdims=True))
        weights = jnp.where(visible, jnp.exp(scores - row_peak), jnp.float32(0.0))
        row_total = lax.optimization_barrier(jnp.sum(weights, axis=1, keepdims=True))
        summed = jnp.dot(weights.astype(jnp.bfloat16), value_rows, preferred_element_type=jnp.float32)
        return (summed / row_total).astype(jnp.bfloat16)
    heads_out = lax.map(head_block, jnp.arange(HEADS * block_count, dtype=jnp.int32))
    attended = heads_out.reshape(HEADS, block_count, block_rows, HD).transpose(1, 2, 0, 3).reshape(TOKENS, HEADS * HD)
    width = TD_DEV + 2 * HALO
    padded = jnp.pad(teacher_rows, ((HALO, HALO), (0, 0)))

    def member_of(shard):
        starts = lax.dynamic_slice(span_start, (shard * S_DEV,), (S_DEV,))
        counts = lax.dynamic_slice(span_len, (shard * S_DEV,), (S_DEV,))
        columns = shard * TD_DEV - HALO + jnp.arange(width, dtype=jnp.int32)
        inside = (columns[None, :] >= starts[:, None]) & (columns[None, :] < (starts + counts)[:, None])
        return (inside.astype(jnp.bfloat16), counts.astype(jnp.float32)[:, None])

    def forward(shard):
        shard = shard.astype(jnp.int32)
        member, counts = member_of(shard)
        window = lax.dynamic_slice(padded, (shard * TD_DEV, jnp.int32(0)), (width, D))
        target = jnp.dot(member, window, preferred_element_type=jnp.float32) / counts
        attended_rows = lax.dynamic_slice(attended, (shard * S_DEV, jnp.int32(0)), (S_DEV, HEADS * HD))
        own_rows = lax.dynamic_slice(student_rows, (shard * S_DEV, jnp.int32(0)), (S_DEV, D))
        student32 = own_rows.astype(jnp.float32) + jnp.dot(attended_rows, out_weight, preferred_element_type=jnp.float32)
        resid = student32 - target
        weighted = (resid / counts).astype(jnp.bfloat16)
        return (student32.astype(jnp.bfloat16), weighted)
    outs_rows, weighted_all = lax.map(forward, jnp.arange(N_CTX, dtype=jnp.int32))
    student_out = outs_rows.reshape(TOKENS, D)

    def spread(shard):
        member, counts = member_of(shard)
        return lax.dot_general(member, weighted_all[shard], (((0,), (0,)), ((), ())), preferred_element_type=jnp.float32)

    def backward(shard):
        shard = shard.astype(jnp.int32)
        own_terms = spread(shard)
        above = spread(jnp.minimum(shard + 1, N_CTX - 1)) * (shard + 1 < N_CTX).astype(jnp.float32)
        below = spread(jnp.maximum(shard - 1, 0)) * (shard > 0).astype(jnp.float32)
        core = own_terms[HALO:HALO + TD_DEV]
        core = core.at[TD_DEV - HALO:].add(above[:HALO])
        core = core.at[:HALO].add(below[TD_DEV + HALO:])
        return core.astype(jnp.bfloat16)
    teacher_grad = lax.map(backward, jnp.arange(N_CTX, dtype=jnp.int32)).reshape(TEACH_TOKENS, D)
    return (student_out, teacher_grad)
```

```python
import functools
import math

import jax
import jax.numpy as jnp
from jax import lax
from jax.experimental import pallas as pl
from jax.experimental.pallas import tpu as pltpu
from jax.sharding import PartitionSpec as P

HEADS = 32
KVH = 4
HD = 128
HALO = 8
GROUP = 4

F32 = jnp.float32
BF16 = jnp.bfloat16
floor_score = -1e30
exp2_scale = math.log2(math.e) / math.sqrt(HD)


def shifted(value, axis, steps):
    count = lax.axis_size(axis)
    leading, last = (max(0, -steps), min(count, count - steps))
    return lax.ppermute(value, axis, [(source, source + steps) for source in range(leading, last)])


def swapped(value, axis, bit):
    count = lax.axis_size(axis)
    return lax.ppermute(value, axis, [(source, source ^ bit) for source in range(count)])


def chunk_step(query_ref, head_count, keys, values, state, visible):
    ones = jnp.ones((values.shape[0], HD), BF16)
    values_ones = jnp.concatenate([values, ones], axis=1)

    def product(head):
        return lax.dot_general(
            query_ref[:, head * HD : (head + 1) * HD],
            keys,
            (((1,), (1,)), ((), ())),
            preferred_element_type=F32,
        )

    result = []
    scores = product(0)
    for head in range(head_count):
        following = product(head + 1) if head + 1 < head_count else None
        if visible is not None:
            scores = jnp.where(visible, scores, floor_score)
        top = jnp.max(scores, axis=1, keepdims=True) * exp2_scale
        if state is None:
            peak = top
        else:
            old_peak, accum = state[head]
            peak = jnp.maximum(old_peak, top)
        weights = jnp.exp2(scores * exp2_scale - peak).astype(BF16)
        added = jnp.dot(weights, values_ones, preferred_element_type=F32)
        if state is None:
            accum = added
        else:
            accum = accum * jnp.exp2(old_peak - peak) + added
        result.append((peak, accum))
        scores = following
    return tuple(result)


def own_kernel(heads, pos_ref, query_ref, own_ref, side_ref, other_ref, peak_ref, accum_ref):
    rows = query_ref.shape[0]
    place = pos_ref[0]
    pieces = [own_ref, side_ref, other_ref.at[0], other_ref.at[1]]
    keys = jnp.concatenate([piece[0] for piece in pieces], axis=0)
    values = jnp.concatenate([piece[1] for piece in pieces], axis=0)
    width = keys.shape[0]
    key_at = lax.broadcasted_iota(jnp.int32, (rows, width), 1)
    row_at = lax.broadcasted_iota(jnp.int32, (rows, width), 0) + place * rows
    slot = key_at // rows
    flip = jnp.where(slot == 0, 0, jnp.where(slot == 1, 2, jnp.where(slot == 2, 1, 3)))
    key_pos = (place ^ flip) * rows + key_at % rows
    state = chunk_step(query_ref, heads, keys, values, None, key_pos <= row_at)
    for head in range(heads):
        peak, accum = state[head]
        peak_ref[:, head : head + 1] = peak
        accum_ref[head] = accum


def rest_kernel(heads, pos_ref, query_ref, near_ref, far_ref, peak_ref, accum_ref, out_ref):
    state = tuple((peak_ref[:, head : head + 1], accum_ref[head]) for head in range(heads))

    def step(index, current):
        pieces = [near_ref.at[2 * index], near_ref.at[2 * index + 1]]
        pieces += [far_ref.at[2 * index], far_ref.at[2 * index + 1]]
        keys = jnp.concatenate([piece[0] for piece in pieces], axis=0)
        values = jnp.concatenate([piece[1] for piece in pieces], axis=0)
        return chunk_step(query_ref, heads, keys, values, current, None)

    state = lax.fori_loop(0, pos_ref[1], step, state)
    for head in range(heads):
        accum = state[head][1]
        out_ref[:, head * HD : (head + 1) * HD] = (accum[:, :HD] / accum[:, HD:]).astype(BF16)


VMEM_SPEC = pl.BlockSpec(memory_space=pltpu.VMEM)
SMEM_SPEC = pl.BlockSpec(memory_space=pltpu.SMEM)


def attention_cost(rows, heads, keys):
    return pl.CostEstimate(
        flops=4 * rows * heads * keys * HD * 2,
        transcendentals=rows * heads * keys,
        bytes_accessed=4 * 1024 * 1024,
    )


def attend_own(pos, queries, head, heads, own, side, other):
    rows = queries.shape[0]
    return pl.pallas_call(
        functools.partial(own_kernel, heads),
        grid=(1,),
        in_specs=[
            SMEM_SPEC,
            pl.BlockSpec((rows, heads * HD), lambda i: (0, head)),
            VMEM_SPEC,
            VMEM_SPEC,
            VMEM_SPEC,
        ],
        out_specs=[VMEM_SPEC, VMEM_SPEC],
        out_shape=[
            jax.ShapeDtypeStruct((rows, HD), F32),
            jax.ShapeDtypeStruct((heads, rows, 2 * HD), F32),
        ],
        cost_estimate=attention_cost(rows, heads, GROUP * rows),
        name="attend_own",
    )(pos, queries, own, side, other)


def attend_rest(pos, queries, head, heads, near, far, peak, accum):
    rows = queries.shape[0]
    return pl.pallas_call(
        functools.partial(rest_kernel, heads),
        grid=(1,),
        in_specs=[
            SMEM_SPEC,
            pl.BlockSpec((rows, heads * HD), lambda i: (0, head)),
            VMEM_SPEC,
            VMEM_SPEC,
            VMEM_SPEC,
            VMEM_SPEC,
        ],
        out_specs=VMEM_SPEC,
        out_shape=jax.ShapeDtypeStruct((rows, heads * HD), BF16),
        cost_estimate=attention_cost(rows, heads, 2 * near.shape[0] * rows),
        name="attend_rest",
    )(pos, queries, near, far, peak, accum)


def base_kernel(count, *refs):
    student_ref, out_ref = refs[1], refs[-1]
    total = student_ref[...].astype(F32)
    for index in range(count):
        total += jnp.dot(refs[2 + index][...], refs[2 + count + index][...], preferred_element_type=F32)
    out_ref[...] = total


def weight_specs(depth, cols, count):
    return [
        pl.BlockSpec((depth, cols), functools.partial(lambda k, j, at: (at[k], j), k))
        for k in range(count)
    ]


def project_own(at, student, pieces, out_weight):
    rows, width = student.shape
    count, depth = len(pieces), pieces[0].shape[1]
    cols = min(512, width)
    return pl.pallas_call(
        functools.partial(base_kernel, count),
        grid_spec=pltpu.PrefetchScalarGridSpec(
            num_scalar_prefetch=1,
            grid=(width // cols,),
            in_specs=[pl.BlockSpec((rows, cols), lambda j, at: (0, j))]
            + [pl.BlockSpec((rows, depth), lambda j, at: (0, 0))] * count
            + weight_specs(depth, cols, count),
            out_specs=pl.BlockSpec((rows, cols), lambda j, at: (0, j)),
        ),
        out_shape=jax.ShapeDtypeStruct((rows, width), F32),
        cost_estimate=pl.CostEstimate(
            flops=2 * rows * width * depth * count,
            transcendentals=0,
            bytes_accessed=2 * depth * count * width + 6 * rows * width,
        ),
        name="project_own",
    )(at, student, *pieces, *([out_weight] * count))


def final_kernel(count, *refs):
    at_ref, start_col, len_col, start_row, len_row, base_ref, teacher_ref, halo_ref = refs[:8]
    piece_refs = refs[8 : 8 + count]
    weight_refs = refs[8 + count : 8 + 2 * count]
    student_ref, core_ref, edge_ref, rim_ref = refs[8 + 2 * count : 12 + 2 * count]
    inner, inner_t, outer, outer_t = refs[12 + 2 * count :]
    rows = base_ref.shape[0]
    teach = teacher_ref.shape[0]

    @pl.when(pl.program_id(0) == 0)
    def _():
        def inside(starts, lens, columns):
            return ((columns >= starts) & (columns < starts + lens)).astype(F32).astype(BF16)

        inner[...] = inside(
            start_col[...], len_col[...], lax.broadcasted_iota(jnp.int32, (rows, teach), 1)
        )
        inner_t[...] = inside(
            start_row[...], len_row[...], lax.broadcasted_iota(jnp.int32, (teach, rows), 0)
        )
        wide = lax.broadcasted_iota(jnp.int32, (rows, 2 * HALO), 1)
        wide = jnp.where(wide < HALO, wide - HALO, wide - HALO + teach)
        outer[...] = inside(start_col[...], len_col[...], wide)
        tall = lax.broadcasted_iota(jnp.int32, (2 * HALO, rows), 0)
        tall = jnp.where(tall < HALO, tall - HALO, tall - HALO + teach)
        outer_t[...] = inside(start_row[...], len_row[...], tall)

    counts = len_col[...].astype(F32)
    target = jnp.dot(inner[...], teacher_ref[...], preferred_element_type=F32)
    target += jnp.dot(outer[...], halo_ref[...], preferred_element_type=F32)
    target = target / counts
    total = base_ref[...]
    for index in range(count):
        total += jnp.dot(piece_refs[index][...], weight_refs[index][...], preferred_element_type=F32)
    student_ref[...] = total.astype(BF16)
    weighted = ((total - target) / counts).astype(BF16)
    core = jnp.dot(inner_t[...], weighted, preferred_element_type=F32)
    core_ref[...] = core.astype(BF16)
    rim_ref[:HALO] = core[:HALO]
    rim_ref[HALO:] = core[teach - HALO :]
    edge_ref[...] = jnp.dot(outer_t[...], weighted, preferred_element_type=F32).astype(BF16)


def finish(at, starts, lens, base, teacher, halo, pieces, out_weight):
    rows, width = base.shape
    teach = teacher.shape[0]
    count, depth = len(pieces), pieces[0].shape[1]
    cols = min(512, width)
    fixed = lambda shape: pl.BlockSpec(shape, lambda j, at: (0, 0))
    column = lambda height: pl.BlockSpec((height, cols), lambda j, at: (0, j))
    return pl.pallas_call(
        functools.partial(final_kernel, count),
        grid_spec=pltpu.PrefetchScalarGridSpec(
            num_scalar_prefetch=1,
            grid=(width // cols,),
            in_specs=[fixed((rows, 1)), fixed((rows, 1)), fixed((1, rows)), fixed((1, rows))]
            + [column(rows), column(teach), column(2 * HALO)]
            + [fixed((rows, depth))] * count
            + weight_specs(depth, cols, count),
            out_specs=[column(rows), column(teach), column(2 * HALO), column(2 * HALO)],
            scratch_shapes=[
                pltpu.VMEM((rows, teach), BF16),
                pltpu.VMEM((teach, rows), BF16),
                pltpu.VMEM((rows, 2 * HALO), BF16),
                pltpu.VMEM((2 * HALO, rows), BF16),
            ],
        ),
        out_shape=[
            jax.ShapeDtypeStruct((rows, width), BF16),
            jax.ShapeDtypeStruct((teach, width), BF16),
            jax.ShapeDtypeStruct((2 * HALO, width), BF16),
            jax.ShapeDtypeStruct((2 * HALO, width), F32),
        ],
        cost_estimate=pl.CostEstimate(
            flops=2 * rows * width * (depth * count + 2 * teach),
            transcendentals=0,
            bytes_accessed=2 * depth * count * width + 6 * rows * width + 4 * teach * width,
        ),
        name="finish",
    )(
        at,
        starts[:, None],
        lens[:, None],
        starts[None, :],
        lens[None, :],
        base,
        teacher,
        halo,
        *pieces,
        *([out_weight] * count),
    )


def body(student_rows, queries, keys_values, out_weight, teacher_rows, span_start, span_len):
    ctx_rank = lax.axis_index("ctx")
    ctx_count = lax.axis_size("ctx")
    tp_lane = lax.axis_index("tp")
    tp_count = lax.axis_size("tp")
    teach_dev = teacher_rows.shape[0]
    heads_dev = queries.shape[1] // HD
    group_size = HEADS // KVH
    kv_dev = max(1, heads_dev // group_size)
    per_own = heads_dev // kv_dev
    groups = ctx_count // GROUP
    before = shifted(teacher_rows[teach_dev - HALO :], "ctx", 1)
    after = shifted(teacher_rows[:HALO], "ctx", -1)
    halo = jnp.concatenate([before, after], axis=0)
    kv_first = tp_lane * heads_dev // group_size
    pos = jnp.stack([ctx_rank % GROUP, ctx_rank // GROUP]).astype(jnp.int32)

    attended = []
    for kv in range(kv_dev):
        own = lax.dynamic_slice_in_dim(keys_values, (kv_first + kv) * HD, HD, 2)
        side = swapped(own, "ctx", 2)
        near = []
        for step in range(1, groups):
            lower = shifted(own, "ctx", GROUP * step)
            near += [lower, swapped(lower, "ctx", 2)]
        near = jnp.stack(near)
        other = swapped(jnp.stack([own, side]), "ctx", 1)
        far = swapped(near, "ctx", 1)
        peak, accum = attend_own(pos, queries, kv, per_own, own, side, other)
        attended.append(attend_rest(pos, queries, kv, per_own, near, far, peak, accum))

    base = project_own(
        jnp.stack([tp_lane * kv_dev + kv for kv in range(kv_dev)]).astype(jnp.int32),
        student_rows,
        attended,
        out_weight,
    )
    pieces, places = [], []
    for step in range(1, tp_count):
        ring = [(i, (i + step) % tp_count) for i in range(tp_count)]
        for kv in range(kv_dev):
            pieces.append(lax.ppermute(attended[kv], "tp", ring))
            places.append((tp_lane - step) % tp_count * kv_dev + kv)
    student_out, core, edge, rim = finish(
        jnp.stack(places).astype(jnp.int32),
        span_start - ctx_rank * teach_dev,
        span_len,
        base,
        teacher_rows,
        halo,
        pieces,
        out_weight,
    )
    from_above = shifted(edge[:HALO], "ctx", -1).astype(F32)
    from_below = shifted(edge[HALO:], "ctx", 1).astype(F32)
    top = (rim[:HALO] + from_below).astype(BF16)
    bottom = (rim[HALO:] + from_above).astype(BF16)
    core = lax.dynamic_update_slice_in_dim(core, top, 0, 0)
    core = lax.dynamic_update_slice_in_dim(core, bottom, teach_dev - HALO, 0)
    return (student_out, core)


def solution(mesh):
    return jax.shard_map(
        body,
        mesh=mesh,
        in_specs=(
            P("ctx", "tp"),
            P("ctx", "tp"),
            P(None, "ctx", None),
            P(None, "tp"),
            P("ctx", "tp"),
            P("ctx"),
            P("ctx"),
        ),
        out_specs=(P("ctx", "tp"), P("ctx", "tp")),
        check_vma=False,
    )
```

```python
import functools
import math

import jax
import jax.numpy as jnp
from jax import lax
from jax.experimental import pallas as pl
from jax.experimental.pallas import tpu as pltpu
from jax.sharding import PartitionSpec as P


HEADS = 32
KVH = 4
HD = 128
HALO = 8
GROUP = 4

F32 = jnp.float32
BF16 = jnp.bfloat16
floor_score = -1e30
exp2_scale = math.log2(math.e) / math.sqrt(HD)

SPLIT = True
ATTN_VMEM = 8 * 1024 * 1024
PROJECT_VMEM = 20 * 1024 * 1024
FINISH_VMEM = 8 * 1024 * 1024


def shifted(value, axis, steps):
    count = lax.axis_size(axis)
    leading, last = (max(0, -steps), min(count, count - steps))
    return lax.ppermute(value, axis, [(source, source + steps) for source in range(leading, last)])


def swapped(value, axis, bit):
    count = lax.axis_size(axis)
    return lax.ppermute(value, axis, [(source, source ^ bit) for source in range(count)])


def attention_step(
    query_ref, heads, keys, values, state, hidden, diagonal, peak_ref, accum_ref
):
    rows = keys[0].shape[0]
    ones = jnp.ones((rows, HD), BF16)
    padded = [jnp.concatenate([block, ones], axis=1) for block in values]

    def product(head):
        query = query_ref[:, head * HD : (head + 1) * HD]
        return [
            lax.dot_general(query, block, (((1,), (1,)), ((), ())), preferred_element_type=F32)
            for block in keys
        ]

    scores = product(0)
    for head in range(heads):
        following = product(head + 1) if head + 1 < heads else None
        if diagonal is not None:
            scores[0] = jnp.where(diagonal, scores[0], floor_score)
        if hidden is None:
            top = functools.reduce(jnp.maximum, scores)
            top = jnp.max(top, axis=1, keepdims=True) * exp2_scale
        else:
            tops = [
                jnp.max(block, axis=1, keepdims=True) * exp2_scale - off
                for block, off in zip(scores, hidden)
            ]
            top = functools.reduce(jnp.maximum, tops)
        peak = top if state is None else jnp.maximum(state[head][0], top)
        accum = None if state is None else state[head][1][...] * jnp.exp2(state[head][0] - peak)
        for index, (block, value) in enumerate(zip(scores, padded)):
            shift = peak if hidden is None else peak + hidden[index]
            weights = jnp.exp2(block * exp2_scale - shift).astype(BF16)
            added = jnp.dot(weights, value, preferred_element_type=F32)
            accum = added if accum is None else accum + added
        peak_ref[:, head : head + 1] = peak
        accum_ref[head] = accum
        scores = following


def own_kernel(heads, query_ref, own_ref, side_ref, other_ref, peak_ref, accum_ref):
    rows = query_ref.shape[0]
    place = lax.rem(lax.axis_index("ctx"), GROUP)
    pieces = [own_ref, side_ref, other_ref.at[0], other_ref.at[1]]
    hidden = [0.0] + [
        jnp.where((place ^ flip) < place, 0.0, -floor_score).astype(F32) for flip in (2, 1, 3)
    ]
    diagonal = lax.broadcasted_iota(jnp.int32, (rows, rows), 1) <= lax.broadcasted_iota(
        jnp.int32, (rows, rows), 0
    )
    attention_step(
        query_ref,
        heads,
        [p[0] for p in pieces],
        [p[1] for p in pieces],
        None,
        hidden,
        diagonal,
        peak_ref,
        accum_ref,
    )


def more_kernel(heads, stages, last, query_ref, near_ref, far_ref, *refs):
    peak_in, accum_in = refs[:2]
    peak_ref, accum_ref = refs[-2:]
    out_ref = refs[2]
    for head in range(heads):
        accum_ref[head] = accum_in[head]
    peak_ref[...] = peak_in[...]
    group = lax.div(lax.axis_index("ctx"), GROUP)
    count = len(stages)

    def step(index, carry):
        @pl.when((group ^ (index + stages[0])) < group)
        def _():
            pieces = [ref.at[at] for ref in (near_ref, far_ref) for at in (index, index + count)]
            state = [(peak_ref[:, head : head + 1], accum_ref.at[head]) for head in range(heads)]
            attention_step(
                query_ref,
                heads,
                [p[0] for p in pieces],
                [p[1] for p in pieces],
                state,
                None,
                None,
                peak_ref,
                accum_ref,
            )

        return carry

    lax.fori_loop(0, count, step, 0)
    if last:
        for head in range(heads):
            accum = accum_ref[head]
            out_ref[:, head * HD : (head + 1) * HD] = (accum[:, :HD] / accum[:, HD:]).astype(BF16)


VMEM_SPEC = pl.BlockSpec(memory_space=pltpu.VMEM)
HBM_SPEC = pl.BlockSpec(memory_space=pltpu.HBM)
MIB = 1024 * 1024


def attention_cost(rows, heads, keys):
    return pl.CostEstimate(
        flops=4 * rows * heads * keys * HD * 2,
        transcendentals=rows * heads * keys,
        bytes_accessed=2 * MIB,
    )


def state_shapes(rows, heads):
    return [((rows, HD), F32), ((heads, rows, 2 * HD), F32)]


def query_spec(rows, heads, kv):
    return pl.BlockSpec((rows, heads * HD), lambda i: (0, kv))


def attend_own(queries, kv, heads, own, side, other):
    rows = queries.shape[0]
    return pl.pallas_call(
        functools.partial(own_kernel, heads),
        grid=(1,),
        in_specs=[query_spec(rows, heads, kv)] + [VMEM_SPEC] * 3,
        out_specs=[VMEM_SPEC] * 2,
        out_shape=[jax.ShapeDtypeStruct(*shape) for shape in state_shapes(rows, heads)],
        compiler_params=pltpu.CompilerParams(vmem_limit_bytes=ATTN_VMEM),
        cost_estimate=attention_cost(rows, heads, GROUP * rows),
        name="attend_own",
    )(queries, own, side, other)


def attend_more(queries, kv, heads, stages, last, near, far, state):
    rows = queries.shape[0]
    states = state_shapes(rows, heads)
    result = [((rows, heads * HD), BF16)] if last else states
    return pl.pallas_call(
        functools.partial(more_kernel, heads, stages, last),
        grid=(1,),
        in_specs=[query_spec(rows, heads, kv)] + [VMEM_SPEC] * 4,
        out_specs=[VMEM_SPEC] * len(result),
        out_shape=[jax.ShapeDtypeStruct(*shape) for shape in result],
        scratch_shapes=[pltpu.VMEM(*shape) for shape in states] if last else [],
        compiler_params=pltpu.CompilerParams(vmem_limit_bytes=ATTN_VMEM),
        cost_estimate=attention_cost(rows, heads, 2 * near.shape[0] * rows),
        name="attend_last" if last else "attend_more",
    )(queries, near, far, *state)


def upright(row):
    count = row.shape[1]
    same = iota((count, count), 0) == iota((count, count), 1)
    return jnp.sum(jnp.where(same, row, 0), axis=1, keepdims=True)


def member_of(starts, lens, columns):
    return ((columns >= starts) & (columns < starts + lens)).astype(F32).astype(BF16)


def iota(shape, axis):
    return lax.broadcasted_iota(jnp.int32, shape, axis)


def rim_rows(index, teach):
    return jnp.where(index < HALO, index - HALO, index - HALO + teach)


def base_kernel(count, cols, slots, tp_count, start_ref, len_ref, student_ref, teacher_ref, halo_ref, *refs):
    piece_refs = refs[:count]
    weight_hbm, base_ref, target_ref, last_ref, buf, sems, last_sem = refs[count:]
    rows, width = student_ref.shape
    teach = teacher_ref.shape[0]
    depth = piece_refs[0].shape[1]
    steps = width // cols

    own = (count + 1) // tp_count

    def block(index):
        lane = lax.rem(lax.axis_index("tp") + tp_count - index // own, tp_count)
        return pl.ds(pl.multiple_of((lane * own + index % own) * depth, depth), depth)

    def loads(step):
        slot = step % slots
        return [
            pltpu.make_async_copy(
                weight_hbm.at[block(index), pl.ds(step * cols, cols)],
                buf.at[slot, index],
                sems.at[slot, index],
            )
            for index in range(count)
        ]

    tail = pltpu.make_async_copy(weight_hbm.at[block(count), :], last_ref, last_sem)
    for step in range(min(slots, steps)):
        for load in loads(step):
            load.start()
    if steps <= slots:
        tail.start()
    starts = upright(start_ref[...]) - lax.axis_index("ctx") * teach
    lens = upright(len_ref[...])
    inner = member_of(starts, lens, iota((rows, teach), 1))
    outer = member_of(starts, lens, rim_rows(iota((rows, 2 * HALO), 1), teach))
    counts = lens.astype(F32)
    for step in range(steps):
        span = slice(step * cols, (step + 1) * cols)
        target = jnp.dot(inner, teacher_ref[:, span], preferred_element_type=F32)
        target += jnp.dot(outer, halo_ref[:, span], preferred_element_type=F32)
        target_ref[:, span] = target / counts
        for load in loads(step):
            load.wait()
        total = student_ref[:, span].astype(F32)
        for index in range(count):
            total += jnp.dot(
                piece_refs[index][...], buf[step % slots, index], preferred_element_type=F32
            )
        base_ref[:, span] = total
        if step + slots < steps:
            for load in loads(step + slots):
                load.start()
            if step + slots == steps - 1:
                tail.start()
    tail.wait()


def project_base(tp_count, starts, lens, student, teacher, halo, pieces, out_weight):
    rows, width = student.shape
    count, depth = len(pieces), pieces[0].shape[1]
    cols, slots = min(512, width), 4
    return pl.pallas_call(
        functools.partial(base_kernel, count, cols, slots, tp_count),
        in_specs=[VMEM_SPEC] * (count + 5) + [HBM_SPEC],
        out_specs=[VMEM_SPEC] * 3,
        out_shape=[jax.ShapeDtypeStruct((rows, width), F32)] * 2
        + [pltpu.VMEM((depth, width), BF16)],
        scratch_shapes=[
            pltpu.VMEM((slots, count, depth, cols), BF16),
            pltpu.SemaphoreType.DMA((slots, count)),
            pltpu.SemaphoreType.DMA,
        ],
        compiler_params=pltpu.CompilerParams(vmem_limit_bytes=PROJECT_VMEM),
        cost_estimate=pl.CostEstimate(
            flops=2 * rows * width * (depth * count + teacher.shape[0]),
            transcendentals=0,
            bytes_accessed=2 * depth * count * width + 10 * rows * width,
        ),
        name="project_base",
    )(starts[None, :], lens[None, :], student, teacher, halo, *pieces, out_weight)


def final_kernel(count, cols, start_ref, len_ref, base_ref, target_ref, *refs):
    piece_refs, weight_refs = refs[:count], refs[count : 2 * count]
    student_out, core_out, edge_ref, rim_ref, student_buf, core_buf, sems = refs[2 * count :]
    rows, width = base_ref.shape
    teach = core_buf.shape[0]
    starts, lens = start_ref[...] - lax.axis_index("ctx") * teach, len_ref[...]
    inner_t = member_of(starts, lens, iota((teach, rows), 0))
    outer_t = member_of(starts, lens, rim_rows(iota((2 * HALO, rows), 0), teach))
    counts = upright(lens).astype(F32)
    copies = []
    for index, start in enumerate(range(0, width, cols)):
        span = slice(start, start + cols)
        total = base_ref[:, span]
        for piece in range(count):
            total += jnp.dot(
                piece_refs[piece][...], weight_refs[piece][:, span], preferred_element_type=F32
            )
        student_buf[:, span] = total.astype(BF16)
        weighted = ((total - target_ref[:, span]) / counts).astype(BF16)
        edge = jnp.dot(outer_t, weighted, preferred_element_type=F32)
        edge_ref[:, span] = edge.astype(BF16)
        core = jnp.dot(inner_t, weighted, preferred_element_type=F32)
        core_buf[:, span] = core.astype(BF16)
        rim_ref[:HALO, span] = core[:HALO]
        rim_ref[HALO:, span] = core[teach - HALO :]
        for slot, (source, result) in enumerate(((student_buf, student_out), (core_buf, core_out))):
            copy = pltpu.make_async_copy(
                source.at[:, span], result.at[:, span], sems.at[slot, index]
            )
            copy.start()
            copies.append(copy)
    for copy in copies:
        copy.wait()


def finish(starts, lens, base, target, teach, pieces, weights):
    rows, width = base.shape
    count, depth = len(pieces), pieces[0].shape[1]
    cols = min(512, width)
    return pl.pallas_call(
        functools.partial(final_kernel, count, cols),
        in_specs=[VMEM_SPEC] * (4 + 2 * count),
        out_specs=[HBM_SPEC, HBM_SPEC, VMEM_SPEC, VMEM_SPEC],
        scratch_shapes=[
            pltpu.VMEM((rows, width), BF16),
            pltpu.VMEM((teach, width), BF16),
            pltpu.SemaphoreType.DMA((2, width // cols)),
        ],
        out_shape=[
            jax.ShapeDtypeStruct((rows, width), BF16),
            jax.ShapeDtypeStruct((teach, width), BF16),
            jax.ShapeDtypeStruct((2 * HALO, width), BF16),
            jax.ShapeDtypeStruct((2 * HALO, width), F32),
        ],
        compiler_params=pltpu.CompilerParams(vmem_limit_bytes=FINISH_VMEM),
        cost_estimate=pl.CostEstimate(
            flops=2 * rows * width * (depth * count + teach),
            transcendentals=0,
            bytes_accessed=2 * depth * count * width + 10 * rows * width + 2 * teach * width,
        ),
        name="finish",
    )(starts[None, :], lens[None, :], base, target, *pieces, *weights)


def rim_kernel(core_ref, rim_ref, below_ref, above_ref, out_ref):
    block = core_ref[...].astype(F32)

    @pl.when(pl.program_id(0) == 0)
    def _():
        first = rim_ref[:HALO] + below_ref[...].astype(F32)
        out_ref[...] = jnp.concatenate([first, block[HALO:]], axis=0).astype(BF16)

    @pl.when(pl.program_id(0) == 1)
    def _():
        last = rim_ref[HALO:] + above_ref[...].astype(F32)
        out_ref[...] = jnp.concatenate([block[:HALO], last], axis=0).astype(BF16)


def add_rim(core, rim, below, above):
    teach, width = core.shape
    end = teach // (2 * HALO) - 1
    place = pl.BlockSpec((2 * HALO, width), lambda i: (i * end, 0))
    return pl.pallas_call(
        rim_kernel,
        grid=(2,),
        in_specs=[place] + [pl.BlockSpec((n, width), lambda i: (0, 0)) for n in (2 * HALO, HALO, HALO)],
        out_specs=place,
        out_shape=jax.ShapeDtypeStruct(core.shape, core.dtype),
        input_output_aliases={0: 0},
        compiler_params=pltpu.CompilerParams(vmem_limit_bytes=4 * MIB),
        name="add_rim",
    )(core, rim, below, above)


def body(student_rows, queries, keys_values, out_weight, teacher_rows, span_start, span_len):
    ctx_count = lax.axis_size("ctx")
    tp_lane = lax.axis_index("tp")
    tp_count = lax.axis_size("tp")
    teach_dev = teacher_rows.shape[0]
    heads_dev = queries.shape[1] // HD
    group_size = HEADS // KVH
    kv_dev = max(1, heads_dev // group_size)
    per_own = heads_dev // kv_dev
    groups = ctx_count // GROUP
    kv_first = tp_lane * heads_dev // group_size

    owns = [
        lax.dynamic_slice_in_dim(keys_values, (kv_first + kv) * HD, HD, 2) for kv in range(kv_dev)
    ]
    both = jnp.stack(owns)
    side_all = swapped(both, "ctx", 2)
    other_all = swapped(jnp.stack([both, side_all], axis=1), "ctx", 1)
    before = shifted(teacher_rows[teach_dev - HALO :], "ctx", 1)
    after = shifted(teacher_rows[:HALO], "ctx", -1)
    halo = jnp.concatenate([before, after], axis=0)

    plan = [list(range(1, groups - 1)), [groups - 1]] if SPLIT else [list(range(1, groups))]
    out_weight = pltpu.with_memory_space_constraint(out_weight, pltpu.HBM)
    attended = []
    for kv in range(kv_dev):
        lifts = []
        for step in range(1, groups):
            lifts.append(swapped(owns[kv], "ctx", GROUP * step))
        state = attend_own(queries, kv, per_own, owns[kv], side_all[kv], other_all[kv])
        for turn, stages in enumerate(plan):
            straight = jnp.stack([lifts[step - 1] for step in stages])
            crossed = swapped(straight, "ctx", 2)
            near = jnp.concatenate([straight, crossed])
            far = swapped(near, "ctx", 1)
            last = turn == len(plan) - 1
            state = attend_more(queries, kv, per_own, stages, last, near, far, state)
        attended.append(state[0])

    pieces = list(attended)
    for step in range(1, tp_count):
        ring = [(i, (i + step) % tp_count) for i in range(tp_count)]
        for kv in range(kv_dev):
            pieces.append(lax.ppermute(attended[kv], "tp", ring))
    base, target, weight = project_base(
        tp_count, span_start, span_len, student_rows, teacher_rows, halo, pieces[:-1], out_weight
    )
    student_out, core, edge, rim = finish(
        span_start, span_len, base, target, teach_dev, pieces[-1:], [weight]
    )
    above = shifted(edge[:HALO], "ctx", -1)
    below = shifted(edge[HALO:], "ctx", 1)
    return (student_out, add_rim(core, rim, below, above))


def solution(mesh):
    return jax.shard_map(
        body,
        mesh=mesh,
        in_specs=(
            P("ctx", "tp"),
            P("ctx", "tp"),
            P(None, "ctx", None),
            P(None, "tp"),
            P("ctx", "tp"),
            P("ctx"),
            P("ctx"),
        ),
        out_specs=(P("ctx", "tp"), P("ctx", "tp")),
        check_vma=False,
    )
```

```python
import functools
import math

import jax
import jax.numpy as jnp
from jax import lax
from jax.experimental import pallas as pl
from jax.experimental.pallas import tpu as pltpu
from jax.sharding import PartitionSpec as P


HEADS = 32
KVH = 4
HD = 128
HALO = 8
GROUP = 4

F32 = jnp.float32
BF16 = jnp.bfloat16
floor_score = -1e30
exp2_scale = math.log2(math.e) / math.sqrt(HD)

ATTN_VMEM = 9 * 1024 * 1024
PROJECT_VMEM = 20 * 1024 * 1024
FINISH_VMEM = 8 * 1024 * 1024


def odd_swapped(value, axis):
    count = lax.axis_size(axis)
    return lax.ppermute(
        value, axis, [(i, i + 1 if i % 2 else i - 1) for i in range(1, count - 1)]
    )


def swapped(value, axis, bit):
    count = lax.axis_size(axis)
    return lax.ppermute(value, axis, [(source, source ^ bit) for source in range(count)])


def attention_step(
    query_ref, heads, keys, values, state, hidden, diagonal, peak_ref, accum_ref
):
    rows = keys[0].shape[0]
    ones = jnp.ones((rows, HD), BF16)
    padded = [jnp.concatenate([block, ones], axis=1) for block in values]

    def product(head):
        query = query_ref[:, head * HD : (head + 1) * HD]
        return [
            lax.dot_general(query, block, (((1,), (1,)), ((), ())), preferred_element_type=F32)
            for block in keys
        ]

    scores = product(0)
    for head in range(heads):
        following = product(head + 1) if head + 1 < heads else None
        if diagonal is not None:
            scores[0] = jnp.where(diagonal, scores[0], floor_score)
        if hidden is None:
            top = functools.reduce(jnp.maximum, scores)
            top = jnp.max(top, axis=1, keepdims=True) * exp2_scale
        else:
            tops = [
                jnp.max(block, axis=1, keepdims=True) * exp2_scale - off
                for block, off in zip(scores, hidden)
            ]
            top = functools.reduce(jnp.maximum, tops)
        peak = top if state is None else jnp.maximum(state[head][0], top)
        accum = None if state is None else state[head][1][...] * jnp.exp2(state[head][0] - peak)
        for index, (block, value) in enumerate(zip(scores, padded)):
            shift = peak if hidden is None else peak + hidden[index]
            weights = jnp.exp2(block * exp2_scale - shift).astype(BF16)
            added = jnp.dot(weights, value, preferred_element_type=F32)
            accum = added if accum is None else accum + added
        peak_ref[:, head : head + 1] = peak
        accum_ref[head] = accum
        scores = following


def own_kernel(heads, query_ref, own_ref, side_ref, other_ref, peak_ref, accum_ref):
    rows = query_ref.shape[0]
    place = lax.rem(lax.axis_index("ctx"), GROUP)
    pieces = [own_ref, side_ref, other_ref.at[0], other_ref.at[1]]
    hidden = [0.0] + [
        jnp.where((place ^ flip) < place, 0.0, -floor_score).astype(F32) for flip in (2, 1, 3)
    ]
    diagonal = lax.broadcasted_iota(jnp.int32, (rows, rows), 1) <= lax.broadcasted_iota(
        jnp.int32, (rows, rows), 0
    )
    attention_step(
        query_ref,
        heads,
        [p[0] for p in pieces],
        [p[1] for p in pieces],
        None,
        hidden,
        diagonal,
        peak_ref,
        accum_ref,
    )


def weight_rows(step, start, depth, lane_rows, tp_count):
    lane = lax.rem(lax.axis_index("tp") + tp_count - step, tp_count)
    return pl.ds(pl.multiple_of(lane * lane_rows + start, HD), depth)


def more_kernel(heads, first, stages, fetch, query_ref, near_ref, far_ref, *refs):
    (peak_in, accum_in), refs = refs[:2], refs[2:]
    copy = None
    if fetch:
        weight_hbm, out_ref, weight_ref, peak_ref, accum_ref, sem = refs
        copy = pltpu.make_async_copy(weight_hbm.at[weight_rows(*fetch), :], weight_ref, sem)
        copy.start()
    else:
        out_ref, peak_ref, accum_ref = refs
    for head in range(heads):
        accum_ref[head] = accum_in[first + head]
        peak_ref[:, head : head + 1] = peak_in[:, first + head : first + head + 1]
    group = lax.div(lax.axis_index("ctx"), GROUP)
    count = len(stages)

    def step(index, carry):
        @pl.when((group ^ (index + stages[0])) < group)
        def _():
            pieces = [ref.at[at] for ref in (near_ref, far_ref) for at in (index, index + count)]
            state = [(peak_ref[:, head : head + 1], accum_ref.at[head]) for head in range(heads)]
            attention_step(
                query_ref,
                heads,
                [p[0] for p in pieces],
                [p[1] for p in pieces],
                state,
                None,
                None,
                peak_ref,
                accum_ref,
            )

        return carry

    lax.fori_loop(0, count, step, 0)
    for head in range(heads):
        accum = accum_ref[head]
        out_ref[:, head * HD : (head + 1) * HD] = (accum[:, :HD] / accum[:, HD:]).astype(BF16)
    if copy is not None:
        copy.wait()


VMEM_SPEC = pl.BlockSpec(memory_space=pltpu.VMEM)
HBM_SPEC = pl.BlockSpec(memory_space=pltpu.HBM)
MIB = 1024 * 1024


def attention_cost(rows, heads, keys):
    return pl.CostEstimate(
        flops=4 * rows * heads * keys * HD * 2,
        transcendentals=rows * heads * keys,
        bytes_accessed=2 * MIB,
    )


def state_shapes(rows, heads):
    return [((rows, HD), F32), ((heads, rows, 2 * HD), F32)]


def query_spec(rows, heads, kv):
    return pl.BlockSpec((rows, heads * HD), lambda i: (0, kv))


def attend_own(queries, kv, heads, own, side, other):
    rows = queries.shape[0]
    return pl.pallas_call(
        functools.partial(own_kernel, heads),
        grid=(1,),
        in_specs=[query_spec(rows, heads, kv)] + [VMEM_SPEC] * 3,
        out_specs=[VMEM_SPEC] * 2,
        out_shape=[jax.ShapeDtypeStruct(*shape) for shape in state_shapes(rows, heads)],
        compiler_params=pltpu.CompilerParams(vmem_limit_bytes=ATTN_VMEM),
        cost_estimate=attention_cost(rows, heads, GROUP * rows),
        name="attend_own",
    )(queries, own, side, other)


def attend_more(queries, kv, per_own, first, heads, stages, near, far, state, fetch, out_weight):
    rows = queries.shape[0]
    extra = [out_weight] if fetch else []
    return pl.pallas_call(
        functools.partial(more_kernel, heads, first, stages, fetch),
        grid=(1,),
        in_specs=[query_spec(rows, heads, (kv * per_own + first) // heads)]
        + [VMEM_SPEC] * 4
        + [HBM_SPEC] * len(extra),
        out_specs=[VMEM_SPEC] * (1 + len(extra)),
        out_shape=[jax.ShapeDtypeStruct((rows, heads * HD), BF16)]
        + [pltpu.VMEM((fetch[2], out_weight.shape[1]), BF16) for _ in extra],
        scratch_shapes=[pltpu.VMEM(*shape) for shape in state_shapes(rows, heads)]
        + [pltpu.SemaphoreType.DMA] * len(extra),
        compiler_params=pltpu.CompilerParams(vmem_limit_bytes=ATTN_VMEM),
        cost_estimate=attention_cost(rows, heads, 2 * near.shape[0] * rows),
        name="attend_more",
    )(queries, near, far, *state, *extra)


def upright(row):
    count = row.shape[1]
    same = iota((count, count), 0) == iota((count, count), 1)
    return jnp.sum(jnp.where(same, row, 0), axis=1, keepdims=True)


def member_of(starts, lens, columns):
    return ((columns >= starts) & (columns < starts + lens)).astype(F32).astype(BF16)


def iota(shape, axis):
    return lax.broadcasted_iota(jnp.int32, shape, axis)


def is_odd():
    return lax.rem(lax.axis_index("ctx"), 2) == 1


def rim_rows(index, teach):
    below = (index < HALO) == is_odd()
    index = jnp.where(index < HALO, index, index - HALO)
    return jnp.where(below, index - HALO, index + teach)


def streamed(pieces, piece_refs, weight_hbm, lane_rows, tp_count, cols, slots, buf, sems):
    steps = weight_hbm.shape[1] // cols

    def loads(step):
        copies, at = [], 0
        for index, (lane_step, start, depth) in enumerate(pieces):
            copies.append(
                pltpu.make_async_copy(
                    weight_hbm.at[
                        weight_rows(lane_step, start, depth, lane_rows, tp_count),
                        pl.ds(step * cols, cols),
                    ],
                    buf.at[step % slots, pl.ds(at, depth), :],
                    sems.at[step % slots, index],
                )
            )
            at += depth
        return copies

    def begin(step):
        for load in loads(step):
            load.start()

    def product(step, total):
        at = 0
        for load in loads(step):
            load.wait()
        for (_, _, depth), ref in zip(pieces, piece_refs):
            block = buf[step % slots, at : at + depth, :]
            total += jnp.dot(ref[...], block, preferred_element_type=F32)
            at += depth
        if step + slots < steps:
            begin(step + slots)
        return total

    for step in range(min(slots, steps)):
        begin(step)
    return product


def base_kernel(pieces, lane_rows, tp_count, cols, slots, start_ref, len_ref, *refs):
    student_ref, teacher_ref, near_ref, far_ref = refs[:4]
    piece_refs = refs[4 : 4 + len(pieces)]
    weight_hbm, base_ref, target_ref, buf, sems = refs[4 + len(pieces) :]
    product = streamed(
        pieces, piece_refs, weight_hbm, lane_rows, tp_count, cols, slots, buf, sems
    )
    rows, width = student_ref.shape
    teach = teacher_ref.shape[0]
    starts = upright(start_ref[...]) - lax.axis_index("ctx") * teach
    lens = upright(len_ref[...])
    inner = member_of(starts, lens, iota((rows, teach), 1))
    outer = member_of(starts, lens, rim_rows(iota((rows, 2 * HALO), 1), teach))
    counts = lens.astype(F32)
    for step in range(width // cols):
        span = slice(step * cols, (step + 1) * cols)
        target = jnp.dot(inner, teacher_ref[:, span], preferred_element_type=F32)
        halo = [ref[:, span].astype(F32) for ref in (near_ref, far_ref)]
        halo = jnp.concatenate(halo, axis=0).astype(BF16)
        target += jnp.dot(outer, halo, preferred_element_type=F32)
        target_ref[:, span] = target / counts
        base_ref[:, span] = product(step, student_ref[:, span].astype(F32))


def add_kernel(pieces, lane_rows, tp_count, cols, slots, base_ref, *refs):
    piece_refs = refs[: len(pieces)]
    weight_hbm, out_ref, buf, sems = refs[len(pieces) :]
    product = streamed(
        pieces, piece_refs, weight_hbm, lane_rows, tp_count, cols, slots, buf, sems
    )
    for step in range(base_ref.shape[1] // cols):
        span = slice(step * cols, (step + 1) * cols)
        out_ref[:, span] = product(step, base_ref[:, span])


def project(kernel, outputs, pieces, values, lane_rows, tp_count, inputs, out_weight):
    width = out_weight.shape[1]
    cols, slots = min(512, width), 4
    depth = sum(piece[2] for piece in pieces)
    rows = inputs[-1].shape[0] if len(inputs) == 1 else inputs[2].shape[0]
    return pl.pallas_call(
        functools.partial(kernel, pieces, lane_rows, tp_count, cols, slots),
        in_specs=[VMEM_SPEC] * (len(inputs) + len(values)) + [HBM_SPEC],
        out_specs=[VMEM_SPEC] * outputs,
        out_shape=[jax.ShapeDtypeStruct((rows, width), F32)] * outputs,
        scratch_shapes=[
            pltpu.VMEM((slots, max(depth, 16), cols), BF16),
            pltpu.SemaphoreType.DMA((slots, max(1, len(pieces)))),
        ],
        compiler_params=pltpu.CompilerParams(vmem_limit_bytes=PROJECT_VMEM),
        cost_estimate=pl.CostEstimate(
            flops=2 * rows * width * depth,
            transcendentals=0,
            bytes_accessed=2 * depth * width + 10 * rows * width,
        ),
    )(*inputs, *values, out_weight)


def final_kernel(count, cols, teach, start_ref, len_ref, base_ref, target_ref, *refs):
    piece_refs, weight_ref = refs[:count], refs[count]
    student_out, weighted_ref, near_ref, far_ref, student_buf, sems = refs[count + 1 :]
    rows, width = base_ref.shape
    starts, lens = start_ref[...] - lax.axis_index("ctx") * teach, len_ref[...]
    outer_t = member_of(starts, lens, rim_rows(iota((2 * HALO, rows), 0), teach))
    counts = upright(lens).astype(F32)
    copies = []
    for index, start in enumerate(range(0, width, cols)):
        span = slice(start, start + cols)
        total = base_ref[:, span]
        at = 0
        for ref in piece_refs:
            block = weight_ref[at : at + ref.shape[1], span]
            total += jnp.dot(ref[...], block, preferred_element_type=F32)
            at += ref.shape[1]
        student_buf[:, span] = total.astype(BF16)
        copy = pltpu.make_async_copy(
            student_buf.at[:, span], student_out.at[:, span], sems.at[index]
        )
        copy.start()
        copies.append(copy)
        weighted = ((total - target_ref[:, span]) / counts).astype(BF16)
        weighted_ref[:, span] = weighted
        edge = jnp.dot(outer_t, weighted, preferred_element_type=F32)
        near_ref[:, span] = edge[:HALO].astype(BF16)
        far_ref[:, span] = edge[HALO:].astype(BF16)
    for copy in copies:
        copy.wait()


def finish(starts, lens, base, target, teach, pieces, weight):
    rows, width = base.shape
    count, depth = len(pieces), weight.shape[0]
    cols = min(512, width)
    return pl.pallas_call(
        functools.partial(final_kernel, count, cols, teach),
        in_specs=[VMEM_SPEC] * (5 + count),
        out_specs=[HBM_SPEC] + [VMEM_SPEC] * 3,
        scratch_shapes=[pltpu.VMEM((rows, width), BF16), pltpu.SemaphoreType.DMA((width // cols,))],
        out_shape=[
            jax.ShapeDtypeStruct((rows, width), BF16),
            jax.ShapeDtypeStruct((rows, width), BF16),
            jax.ShapeDtypeStruct((HALO, width), BF16),
            jax.ShapeDtypeStruct((HALO, width), BF16),
        ],
        compiler_params=pltpu.CompilerParams(vmem_limit_bytes=FINISH_VMEM),
        cost_estimate=pl.CostEstimate(
            flops=2 * rows * width * depth,
            transcendentals=0,
            bytes_accessed=2 * depth * width + 10 * rows * width,
        ),
        name="finish",
    )(starts[None, :], lens[None, :], base, target, *pieces, weight)


def spread_kernel(cols, start_ref, len_ref, weighted_ref, core_out, rim_ref, core_buf, sems):
    rows, width = weighted_ref.shape
    teach = core_buf.shape[0]
    starts, lens = start_ref[...] - lax.axis_index("ctx") * teach, len_ref[...]
    inner_t = member_of(starts, lens, iota((teach, rows), 0))
    copies = []
    for index, start in enumerate(range(0, width, cols)):
        span = slice(start, start + cols)
        core = jnp.dot(inner_t, weighted_ref[:, span], preferred_element_type=F32)
        core_buf[:, span] = core.astype(BF16)
        rim_ref[: 2 * HALO, span] = core[: 2 * HALO]
        rim_ref[2 * HALO :, span] = core[teach - 2 * HALO :]
        copy = pltpu.make_async_copy(
            core_buf.at[:, span], core_out.at[:, span], sems.at[index]
        )
        copy.start()
        copies.append(copy)
    for copy in copies:
        copy.wait()


def spread_out(starts, lens, weighted, teach):
    rows, width = weighted.shape
    cols = min(1024, width)
    return pl.pallas_call(
        functools.partial(spread_kernel, cols),
        in_specs=[VMEM_SPEC] * 3,
        out_specs=[HBM_SPEC, VMEM_SPEC],
        scratch_shapes=[pltpu.VMEM((teach, width), BF16), pltpu.SemaphoreType.DMA((width // cols,))],
        out_shape=[
            jax.ShapeDtypeStruct((teach, width), BF16),
            jax.ShapeDtypeStruct((4 * HALO, width), F32),
        ],
        compiler_params=pltpu.CompilerParams(vmem_limit_bytes=FINISH_VMEM),
        cost_estimate=pl.CostEstimate(
            flops=2 * rows * width * teach, transcendentals=0, bytes_accessed=2 * teach * width
        ),
        name="spread_out",
    )(starts[None, :], lens[None, :], weighted)


def rim_kernel(core_in, rim_ref, near_ref, far_ref, core_out, block_ref, sems):
    del core_in
    near, far = near_ref[...].astype(F32), far_ref[...].astype(F32)
    rest = jnp.zeros_like(near)
    odd = is_odd()
    first = jnp.concatenate([jnp.where(odd, near, far), rest], axis=0)
    last = jnp.concatenate([rest, jnp.where(odd, far, near)], axis=0)
    height = 2 * HALO
    copies = []
    for slot, (part, row) in enumerate(((first, 0), (last, core_out.shape[0] - height))):
        block_ref[slot] = (rim_ref[slot * height : (slot + 1) * height] + part).astype(BF16)
        copy = pltpu.make_async_copy(
            block_ref.at[slot], core_out.at[pl.ds(row, height), :], sems.at[slot]
        )
        copy.start()
        copies.append(copy)
    for copy in copies:
        copy.wait()


def add_rim(core, rim, near, far):
    width = core.shape[1]
    return pl.pallas_call(
        rim_kernel,
        in_specs=[HBM_SPEC] + [VMEM_SPEC] * 3,
        out_specs=HBM_SPEC,
        out_shape=jax.ShapeDtypeStruct(core.shape, core.dtype),
        scratch_shapes=[pltpu.VMEM((2, 2 * HALO, width), BF16), pltpu.SemaphoreType.DMA((2,))],
        input_output_aliases={0: 0},
        compiler_params=pltpu.CompilerParams(vmem_limit_bytes=4 * MIB),
        name="add_rim",
    )(core, rim, near, far)


def body(student_rows, queries, keys_values, out_weight, teacher_rows, span_start, span_len):
    ctx_count = lax.axis_size("ctx")
    tp_lane = lax.axis_index("tp")
    tp_count = lax.axis_size("tp")
    teach_dev = teacher_rows.shape[0]
    heads_dev = queries.shape[1] // HD
    group_size = HEADS // KVH
    kv_dev = max(1, heads_dev // group_size)
    per_own = heads_dev // kv_dev
    groups = ctx_count // GROUP
    kv_first = tp_lane * heads_dev // group_size

    owns = [
        lax.dynamic_slice_in_dim(keys_values, (kv_first + kv) * HD, HD, 2) for kv in range(kv_dev)
    ]
    place = jnp.where(is_odd(), 0, teach_dev - HALO)
    edges = [
        lax.dynamic_slice_in_dim(teacher_rows, start, HALO, 0)
        for start in (place, teach_dev - HALO - place)
    ]
    owns, edges = lax.optimization_barrier((owns, edges))
    halos = [swapped(edges[0], "ctx", 1)]
    halos.append(odd_swapped(edges[1], "ctx"))
    both = jnp.stack(owns)
    side_all = swapped(both, "ctx", 2)
    other_all = swapped(jnp.stack([both, side_all], axis=1), "ctx", 1)
    stages = list(range(1, groups))
    lane_rows = heads_dev * HD
    out_weight = pltpu.with_memory_space_constraint(out_weight, pltpu.HBM)
    attended = []
    for kv in range(kv_dev):
        lifts = []
        for step in range(1, groups):
            lifts.append(swapped(owns[kv], "ctx", GROUP * step))
        state = attend_own(queries, kv, per_own, owns[kv], side_all[kv], other_all[kv])
        straight = jnp.stack(lifts)
        near = jnp.concatenate([straight, swapped(straight, "ctx", 2)])
        far = swapped(near, "ctx", 1)
        final = kv == kv_dev - 1
        parts = 2 if final and per_own % 2 == 0 else 1
        heads = per_own // parts
        for part in range(parts):
            first = part * heads
            fetch = None
            if final and part == 0:
                fetch = (tp_count - 1, kv * per_own * HD, per_own * HD, lane_rows, tp_count)
            result = attend_more(
                queries, kv, per_own, first, heads, stages, near, far, state, fetch, out_weight
            )
            if fetch:
                weight = result[1]
            attended.append((kv, part, (kv * per_own + first) * HD, result[0]))

    early, late, rest = [], [], []
    for kv, part, start, value in attended:
        (late if kv == kv_dev - 1 else early).append(((0, start, value.shape[1]), value))
    for step in range(1, tp_count):
        ring = [(i, (i + step) % tp_count) for i in range(tp_count)]
        for kv, part, start, value in attended:
            got = lax.ppermute(value, "tp", ring)
            if kv == kv_dev - 1 and step == tp_count - 1:
                rest.append(got)
            else:
                late.append(((step, start, value.shape[1]), got))
    spans = (span_start[None, :], span_len[None, :])
    base, target = project(
        base_kernel,
        2,
        [piece for piece, _ in early],
        [value for _, value in early],
        lane_rows,
        tp_count,
        [*spans, student_rows, teacher_rows, *halos],
        out_weight,
    )
    (base,) = project(
        add_kernel,
        1,
        [piece for piece, _ in late],
        [value for _, value in late],
        lane_rows,
        tp_count,
        [base],
        out_weight,
    )
    student_out, weighted, near, far = finish(
        span_start, span_len, base, target, teach_dev, rest, weight
    )
    near = swapped(near, "ctx", 1)
    far = odd_swapped(far, "ctx")
    core, rim = spread_out(span_start, span_len, weighted, teach_dev)
    return (student_out, add_rim(core, rim, near, far))


def solution(mesh):
    return jax.shard_map(
        body,
        mesh=mesh,
        in_specs=(
            P("ctx", "tp"),
            P("ctx", "tp"),
            P(None, "ctx", None),
            P(None, "tp"),
            P("ctx", "tp"),
            P("ctx"),
            P("ctx"),
        ),
        out_specs=(P("ctx", "tp"), P("ctx", "tp")),
        check_vma=False,
    )
```

```python
import functools
import math

import jax
import jax.numpy as jnp
from jax import lax
from jax.experimental import pallas as pl
from jax.experimental.pallas import tpu as pltpu
from jax.sharding import PartitionSpec as P


HEADS = 32
KVH = 4
HD = 128
HALO = 8
GROUP = 4

F32 = jnp.float32
BF16 = jnp.bfloat16
floor_score = -1e30
exp2_scale = math.log2(math.e) / math.sqrt(HD)

ATTN_VMEM = 9 * 1024 * 1024
PROJECT_VMEM = 6 * 1024 * 1024
FINISH_VMEM = 8 * 1024 * 1024


def odd_swapped(value, axis):
    count = lax.axis_size(axis)
    return lax.ppermute(
        value, axis, [(i, i + 1 if i % 2 else i - 1) for i in range(1, count - 1)]
    )


def swapped(value, axis, bit):
    count = lax.axis_size(axis)
    return lax.ppermute(value, axis, [(source, source ^ bit) for source in range(count)])


def attention_step(
    query_ref, heads, keys, values, state, hidden, diagonal, peak_ref, accum_ref
):
    rows = keys[0].shape[0]
    ones = jnp.ones((rows, HD), BF16)
    padded = [jnp.concatenate([block, ones], axis=1) for block in values]

    def product(head):
        query = query_ref[:, head * HD : (head + 1) * HD]
        return [
            lax.dot_general(query, block, (((1,), (1,)), ((), ())), preferred_element_type=F32)
            for block in keys
        ]

    scores = product(0)
    for head in range(heads):
        following = product(head + 1) if head + 1 < heads else None
        if diagonal is not None:
            scores[0] = jnp.where(diagonal, scores[0], floor_score)
        if hidden is None:
            top = functools.reduce(jnp.maximum, scores)
            top = jnp.max(top, axis=1, keepdims=True) * exp2_scale
        else:
            tops = [
                jnp.max(block, axis=1, keepdims=True) * exp2_scale - off
                for block, off in zip(scores, hidden)
            ]
            top = functools.reduce(jnp.maximum, tops)
        peak = top if state is None else jnp.maximum(state[head][0], top)
        accum = None if state is None else state[head][1][...] * jnp.exp2(state[head][0] - peak)
        for index, (block, value) in enumerate(zip(scores, padded)):
            shift = peak if hidden is None else peak + hidden[index]
            weights = jnp.exp2(block * exp2_scale - shift).astype(BF16)
            added = jnp.dot(weights, value, preferred_element_type=F32)
            accum = added if accum is None else accum + added
        peak_ref[:, head : head + 1] = peak
        accum_ref[head] = accum
        scores = following


def own_kernel(heads, query_ref, own_ref, side_ref, other_ref, peak_ref, accum_ref):
    rows = query_ref.shape[0]
    place = lax.rem(lax.axis_index("ctx"), GROUP)
    pieces = [own_ref, side_ref, other_ref.at[0], other_ref.at[1]]
    hidden = [0.0] + [
        jnp.where((place ^ flip) < place, 0.0, -floor_score).astype(F32) for flip in (2, 1, 3)
    ]
    diagonal = lax.broadcasted_iota(jnp.int32, (rows, rows), 1) <= lax.broadcasted_iota(
        jnp.int32, (rows, rows), 0
    )
    attention_step(
        query_ref,
        heads,
        [p[0] for p in pieces],
        [p[1] for p in pieces],
        None,
        hidden,
        diagonal,
        peak_ref,
        accum_ref,
    )


def weight_rows(step, start, depth, lane_rows, tp_count):
    lane = lax.rem(lax.axis_index("tp") + tp_count - step, tp_count)
    return pl.ds(pl.multiple_of(lane * lane_rows + start, HD), depth)


def fetches(blocks, lanes, weight_hbm, refs, sems):
    return [
        pltpu.make_async_copy(weight_hbm.at[weight_rows(*block, *lanes), :], ref, sems.at[index])
        for index, (block, ref) in enumerate(zip(blocks, refs))
    ]


def more_kernel(heads, first, turns, fetch, lanes, query_ref, *refs):
    parts = [(stages, refs[4 * k : 4 * k + 4]) for k, stages in enumerate(turns)]
    refs = refs[4 * len(turns) :]
    (peak_in, accum_in, weight_hbm, out_ref), refs = refs[:4], refs[4:]
    peak_ref, accum_ref, sems = refs[-3:]
    copies = fetches(fetch, lanes, weight_hbm, refs[:-3], sems)
    for copy in copies:
        copy.start()
    for head in range(heads):
        accum_ref[head] = accum_in[first + head]
        peak_ref[:, head : head + 1] = peak_in[:, first + head : first + head + 1]
    group = lax.div(lax.axis_index("ctx"), GROUP)
    for stages, blocks in parts:

        def step(index, carry, stages=stages, blocks=blocks):
            @pl.when((group ^ (index + stages[0])) < group)
            def _():
                pieces = [ref.at[index] for ref in blocks]
                state = [
                    (peak_ref[:, head : head + 1], accum_ref.at[head]) for head in range(heads)
                ]
                attention_step(
                    query_ref,
                    heads,
                    [p[0] for p in pieces],
                    [p[1] for p in pieces],
                    state,
                    None,
                    None,
                    peak_ref,
                    accum_ref,
                )

            return carry

        lax.fori_loop(0, len(stages), step, 0)
    for head in range(heads):
        accum = accum_ref[head]
        out_ref[:, head * HD : (head + 1) * HD] = (accum[:, :HD] / accum[:, HD:]).astype(BF16)
    for copy in copies:
        copy.wait()


VMEM_SPEC = pl.BlockSpec(memory_space=pltpu.VMEM)
HBM_SPEC = pl.BlockSpec(memory_space=pltpu.HBM)
MIB = 1024 * 1024


def attention_cost(rows, heads, keys):
    return pl.CostEstimate(
        flops=4 * rows * heads * keys * HD * 2,
        transcendentals=rows * heads * keys,
        bytes_accessed=2 * MIB,
    )


def state_shapes(rows, heads):
    return [((rows, HD), F32), ((heads, rows, 2 * HD), F32)]


def query_spec(rows, heads, kv):
    return pl.BlockSpec((rows, heads * HD), lambda i: (0, kv))


def attend_own(queries, kv, heads, own, side, other):
    rows = queries.shape[0]
    return pl.pallas_call(
        functools.partial(own_kernel, heads),
        grid=(1,),
        in_specs=[query_spec(rows, heads, kv)] + [VMEM_SPEC] * 3,
        out_specs=[VMEM_SPEC] * 2,
        out_shape=[jax.ShapeDtypeStruct(*shape) for shape in state_shapes(rows, heads)],
        compiler_params=pltpu.CompilerParams(vmem_limit_bytes=ATTN_VMEM),
        cost_estimate=attention_cost(rows, heads, GROUP * rows),
        name="attend_own",
    )(queries, own, side, other)


def fetched(fetch, out_weight):
    return [pltpu.VMEM((depth, out_weight.shape[1]), BF16) for _, _, depth in fetch]


def attend_more(
    queries, kv, per_own, first, heads, turns, blocks, state, fetch, lanes, out_weight
):
    rows = queries.shape[0]
    return pl.pallas_call(
        functools.partial(more_kernel, heads, first, turns, fetch, lanes),
        grid=(1,),
        in_specs=[query_spec(rows, heads, (kv * per_own + first) // heads)]
        + [VMEM_SPEC] * (len(blocks) + 2)
        + [HBM_SPEC],
        out_specs=[VMEM_SPEC] * (1 + len(fetch)),
        out_shape=[jax.ShapeDtypeStruct((rows, heads * HD), BF16)] + fetched(fetch, out_weight),
        scratch_shapes=[pltpu.VMEM(*shape) for shape in state_shapes(rows, heads)]
        + [pltpu.SemaphoreType.DMA((max(1, len(fetch)),))],
        compiler_params=pltpu.CompilerParams(vmem_limit_bytes=ATTN_VMEM),
        cost_estimate=attention_cost(rows, heads, GROUP * len(sum(turns, [])) * rows),
        name="attend_more",
    )(queries, *blocks, *state, out_weight)


def upright(row):
    count = row.shape[1]
    same = iota((count, count), 0) == iota((count, count), 1)
    return jnp.sum(jnp.where(same, row, 0), axis=1, keepdims=True)


def member_of(starts, lens, columns):
    return ((columns >= starts) & (columns < starts + lens)).astype(F32).astype(BF16)


def iota(shape, axis):
    return lax.broadcasted_iota(jnp.int32, shape, axis)


def is_odd():
    return lax.rem(lax.axis_index("ctx"), 2) == 1


def rim_rows(index, teach):
    below = (index < HALO) == is_odd()
    index = jnp.where(index < HALO, index, index - HALO)
    return jnp.where(below, index - HALO, index + teach)


def joined(pieces, piece_refs):
    runs = []
    for (block, start, depth), ref in zip(pieces, piece_refs):
        if runs and runs[-1][0] == block and runs[-1][1] + runs[-1][2] == start:
            runs[-1][2] += depth
            runs[-1][3].append(ref)
        else:
            runs.append([block, start, depth, [ref]])
    return [
        (block, start, depth, jnp.concatenate([ref[...] for ref in refs], axis=1))
        for block, start, depth, refs in runs
    ]


def product(runs, weight_refs, span, total):
    for block, start, depth, value in runs:
        rows = weight_refs[block][start : start + depth, span]
        total += jnp.dot(value, rows, preferred_element_type=F32)
    return total


def base_kernel(pieces, cols, start_ref, len_ref, *refs):
    student_ref, teacher_ref, near_ref, far_ref = refs[:4]
    piece_refs, weight_refs = refs[4 : 4 + len(pieces)], refs[4 + len(pieces) : -2]
    base_ref, target_ref = refs[-2:]
    rows, width = student_ref.shape
    teach = teacher_ref.shape[0]
    starts = upright(start_ref[...]) - lax.axis_index("ctx") * teach
    lens = upright(len_ref[...])
    inner = member_of(starts, lens, iota((rows, teach), 1))
    outer = member_of(starts, lens, rim_rows(iota((rows, 2 * HALO), 1), teach))
    share = 1.0 / lens.astype(F32)
    runs = joined(pieces, piece_refs)
    for step in range(width // cols):
        span = slice(step * cols, (step + 1) * cols)
        target = jnp.dot(inner, teacher_ref[:, span], preferred_element_type=F32)
        halo = [ref[:, span].astype(F32) for ref in (near_ref, far_ref)]
        halo = jnp.concatenate(halo, axis=0).astype(BF16)
        target += jnp.dot(outer, halo, preferred_element_type=F32)
        target_ref[:, span] = target * share
        total = student_ref[:, span].astype(F32)
        base_ref[:, span] = product(runs, weight_refs, span, total)


def late_kernel(pieces, count, fetch, lanes, cols, base_ref, *refs):
    piece_refs, weight_refs = refs[: len(pieces)], refs[len(pieces) : len(pieces) + count]
    weight_hbm, out_ref, last_ref, sems = refs[len(pieces) + count :]
    copies = fetches(fetch, lanes, weight_hbm, [last_ref], sems)
    for copy in copies:
        copy.start()
    runs = joined(pieces, piece_refs)
    for start in range(0, base_ref.shape[1], cols):
        span = slice(start, start + cols)
        out_ref[:, span] = product(runs, weight_refs, span, base_ref[:, span])
    for copy in copies:
        copy.wait()


def product_cost(rows, width, pieces):
    depth = sum(piece[2] for piece in pieces)
    return pl.CostEstimate(
        flops=2 * rows * width * depth,
        transcendentals=0,
        bytes_accessed=2 * depth * width + 10 * rows * width,
    )


def project_base(pieces, values, weights, starts, lens, student, teacher, halos):
    rows, width = student.shape
    return pl.pallas_call(
        functools.partial(base_kernel, pieces, min(512, width)),
        in_specs=[VMEM_SPEC] * (6 + len(values) + len(weights)),
        out_specs=[VMEM_SPEC] * 2,
        out_shape=[jax.ShapeDtypeStruct((rows, width), F32)] * 2,
        compiler_params=pltpu.CompilerParams(vmem_limit_bytes=PROJECT_VMEM),
        cost_estimate=product_cost(rows, width, pieces),
        name="project_base",
    )(starts[None, :], lens[None, :], student, teacher, *halos, *values, *weights)


def project_late(pieces, values, weights, base, fetch, lanes, out_weight):
    rows, width = base.shape
    return pl.pallas_call(
        functools.partial(late_kernel, pieces, len(weights), fetch, lanes, min(512, width)),
        in_specs=[VMEM_SPEC] * (1 + len(values) + len(weights)) + [HBM_SPEC],
        out_specs=[VMEM_SPEC] * 2,
        out_shape=[jax.ShapeDtypeStruct((rows, width), F32)] + fetched(fetch, out_weight),
        scratch_shapes=[pltpu.SemaphoreType.DMA((1,))],
        compiler_params=pltpu.CompilerParams(vmem_limit_bytes=PROJECT_VMEM),
        cost_estimate=product_cost(rows, width, pieces),
        name="project_late",
    )(base, *values, *weights, out_weight)


def final_kernel(count, cols, teach, start_ref, len_ref, base_ref, target_ref, *refs):
    piece_refs, weight_ref = refs[:count], refs[count]
    student_out, weighted_ref, near_ref, far_ref, student_buf, sems = refs[count + 1 :]
    rows, width = base_ref.shape
    starts, lens = start_ref[...] - lax.axis_index("ctx") * teach, len_ref[...]
    outer_t = member_of(starts, lens, rim_rows(iota((2 * HALO, rows), 0), teach))
    share = 1.0 / upright(lens).astype(F32)
    value = jnp.concatenate([ref[...] for ref in piece_refs], axis=1)
    copies = []
    for index, start in enumerate(range(0, width, cols)):
        span = slice(start, start + cols)
        total = base_ref[:, span]
        total += jnp.dot(value, weight_ref[:, span], preferred_element_type=F32)
        student_buf[:, span] = total.astype(BF16)
        copy = pltpu.make_async_copy(
            student_buf.at[:, span], student_out.at[:, span], sems.at[index]
        )
        copy.start()
        copies.append(copy)
        weighted = ((total - target_ref[:, span]) * share).astype(BF16)
        weighted_ref[:, span] = weighted
        edge = jnp.dot(outer_t, weighted, preferred_element_type=F32)
        near_ref[:, span] = edge[:HALO].astype(BF16)
        far_ref[:, span] = edge[HALO:].astype(BF16)
    for copy in copies:
        copy.wait()


def finish(starts, lens, base, target, teach, pieces, weight):
    rows, width = base.shape
    count, depth = len(pieces), weight.shape[0]
    cols = min(512, width)
    return pl.pallas_call(
        functools.partial(final_kernel, count, cols, teach),
        in_specs=[VMEM_SPEC] * (5 + count),
        out_specs=[HBM_SPEC] + [VMEM_SPEC] * 3,
        scratch_shapes=[pltpu.VMEM((rows, width), BF16), pltpu.SemaphoreType.DMA((width // cols,))],
        out_shape=[
            jax.ShapeDtypeStruct((rows, width), BF16),
            jax.ShapeDtypeStruct((rows, width), BF16),
            jax.ShapeDtypeStruct((HALO, width), BF16),
            jax.ShapeDtypeStruct((HALO, width), BF16),
        ],
        compiler_params=pltpu.CompilerParams(vmem_limit_bytes=FINISH_VMEM),
        cost_estimate=pl.CostEstimate(
            flops=2 * rows * width * depth,
            transcendentals=0,
            bytes_accessed=2 * depth * width + 10 * rows * width,
        ),
        name="finish",
    )(starts[None, :], lens[None, :], base, target, *pieces, weight)


def spread_kernel(cols, start_ref, len_ref, weighted_ref, core_out, rim_ref, core_buf, sems):
    rows, width = weighted_ref.shape
    teach = core_buf.shape[0]
    starts, lens = start_ref[...] - lax.axis_index("ctx") * teach, len_ref[...]
    inner_t = member_of(starts, lens, iota((teach, rows), 0))
    copies = []
    for index, start in enumerate(range(0, width, cols)):
        span = slice(start, start + cols)
        core = jnp.dot(inner_t, weighted_ref[:, span], preferred_element_type=F32)
        core_buf[:, span] = core.astype(BF16)
        rim_ref[: 2 * HALO, span] = core[: 2 * HALO]
        rim_ref[2 * HALO :, span] = core[teach - 2 * HALO :]
        copy = pltpu.make_async_copy(
            core_buf.at[:, span], core_out.at[:, span], sems.at[index]
        )
        copy.start()
        copies.append(copy)
    for copy in copies:
        copy.wait()


def spread_out(starts, lens, weighted, teach):
    rows, width = weighted.shape
    cols = min(1024, width)
    return pl.pallas_call(
        functools.partial(spread_kernel, cols),
        in_specs=[VMEM_SPEC] * 3,
        out_specs=[HBM_SPEC, VMEM_SPEC],
        scratch_shapes=[pltpu.VMEM((teach, width), BF16), pltpu.SemaphoreType.DMA((width // cols,))],
        out_shape=[
            jax.ShapeDtypeStruct((teach, width), BF16),
            jax.ShapeDtypeStruct((4 * HALO, width), F32),
        ],
        compiler_params=pltpu.CompilerParams(vmem_limit_bytes=FINISH_VMEM),
        cost_estimate=pl.CostEstimate(
            flops=2 * rows * width * teach, transcendentals=0, bytes_accessed=2 * teach * width
        ),
        name="spread_out",
    )(starts[None, :], lens[None, :], weighted)


def rim_kernel(core_in, rim_ref, near_ref, far_ref, core_out, block_ref, sems):
    del core_in
    near, far = near_ref[...].astype(F32), far_ref[...].astype(F32)
    rest = jnp.zeros_like(near)
    odd = is_odd()
    first = jnp.concatenate([jnp.where(odd, near, far), rest], axis=0)
    last = jnp.concatenate([rest, jnp.where(odd, far, near)], axis=0)
    height = 2 * HALO
    copies = []
    for slot, (part, row) in enumerate(((first, 0), (last, core_out.shape[0] - height))):
        block_ref[slot] = (rim_ref[slot * height : (slot + 1) * height] + part).astype(BF16)
        copy = pltpu.make_async_copy(
            block_ref.at[slot], core_out.at[pl.ds(row, height), :], sems.at[slot]
        )
        copy.start()
        copies.append(copy)
    for copy in copies:
        copy.wait()


def add_rim(core, rim, near, far):
    width = core.shape[1]
    return pl.pallas_call(
        rim_kernel,
        in_specs=[HBM_SPEC] + [VMEM_SPEC] * 3,
        out_specs=HBM_SPEC,
        out_shape=jax.ShapeDtypeStruct(core.shape, core.dtype),
        scratch_shapes=[pltpu.VMEM((2, 2 * HALO, width), BF16), pltpu.SemaphoreType.DMA((2,))],
        input_output_aliases={0: 0},
        compiler_params=pltpu.CompilerParams(vmem_limit_bytes=4 * MIB),
        name="add_rim",
    )(core, rim, near, far)


def body(student_rows, queries, keys_values, out_weight, teacher_rows, span_start, span_len):
    ctx_count = lax.axis_size("ctx")
    tp_lane = lax.axis_index("tp")
    tp_count = lax.axis_size("tp")
    teach_dev = teacher_rows.shape[0]
    heads_dev = queries.shape[1] // HD
    group_size = HEADS // KVH
    kv_dev = max(1, heads_dev // group_size)
    per_own = heads_dev // kv_dev
    groups = ctx_count // GROUP
    kv_first = tp_lane * heads_dev // group_size

    owns = [
        lax.dynamic_slice_in_dim(keys_values, (kv_first + kv) * HD, HD, 2) for kv in range(kv_dev)
    ]
    place = jnp.where(is_odd(), 0, teach_dev - HALO)
    edges = [
        lax.dynamic_slice_in_dim(teacher_rows, start, HALO, 0)
        for start in (place, teach_dev - HALO - place)
    ]
    halos = [swapped(edges[0], "ctx", 1)]
    halos.append(odd_swapped(edges[1], "ctx"))
    both = jnp.stack(owns)
    side_all = swapped(both, "ctx", 2)
    other_all = swapped(jnp.stack([both, side_all], axis=1), "ctx", 1)
    stages = list(range(1, groups))
    lanes = (heads_dev * HD, tp_count)
    depth = per_own * HD
    weights = {}
    out_weight = pltpu.with_memory_space_constraint(out_weight, pltpu.HBM)
    attended = []
    for kv in range(kv_dev):
        lifts = []
        for step in range(1, groups):
            lifts.append(swapped(owns[kv], "ctx", GROUP * step))
        state = attend_own(queries, kv, per_own, owns[kv], side_all[kv], other_all[kv])
        turns = [stages] if kv or len(stages) < 2 else [stages[:1], stages[1:]]
        blocks = []
        for turn, chosen in enumerate(turns):
            straight = jnp.stack([lifts[step - 1] for step in chosen])
            crossed = swapped(straight, "ctx", 2)
            if turn < len(turns) - 1:
                pair = swapped(jnp.concatenate([straight, crossed]), "ctx", 1)
                blocks += [straight, crossed, pair[: len(chosen)], pair[len(chosen) :]]
                continue
            blocks += [straight, crossed, swapped(straight, "ctx", 1)]
            blocks.append(swapped(crossed, "ctx", 1))
        final = kv == kv_dev - 1
        parts = 2 if final and per_own % 2 == 0 else 1
        heads = per_own // parts
        for part in range(parts):
            first = part * heads
            if not final:
                wanted = [(0, kv)]
            else:
                wanted = [(0, kv)] + [
                    (step, other)
                    for step in range(1, tp_count)
                    for other in range(kv_dev)
                    if (step, other) != (tp_count - 1, kv)
                ]
                share = -(-len(wanted) // parts)
                wanted = wanted[part * share : (part + 1) * share]
            fetch = [(step, other * depth, depth) for step, other in wanted]
            result = attend_more(
                queries, kv, per_own, first, heads, turns, blocks, state, fetch, lanes, out_weight
            )
            weights.update(zip(wanted, result[1:]))
            attended.append((kv, part, first * HD, result[0]))

    early, late, rest = [], [], []
    for kv, part, start, value in attended:
        (late if kv == kv_dev - 1 else early).append(((0, kv), start, value))
    for step in range(1, tp_count):
        ring = [(i, (i + step) % tp_count) for i in range(tp_count)]
        for kv, part, start, value in attended:
            got = lax.ppermute(value, "tp", ring)
            if kv == kv_dev - 1 and step == tp_count - 1:
                rest.append(got)
            else:
                late.append(((step, kv), start, got))

    def products(entries):
        blocks = list(dict.fromkeys(block for block, _, _ in entries))
        pieces = [(blocks.index(block), at, value.shape[1]) for block, at, value in entries]
        return pieces, [value for _, _, value in entries], [weights[block] for block in blocks]

    base, target = project_base(
        *products(early), span_start, span_len, student_rows, teacher_rows, halos
    )
    fetch = [(tp_count - 1, (kv_dev - 1) * depth, depth)]
    base, weight = project_late(*products(late), base, fetch, lanes, out_weight)
    student_out, weighted, near, far = finish(
        span_start, span_len, base, target, teach_dev, rest, weight
    )
    near = swapped(near, "ctx", 1)
    far = odd_swapped(far, "ctx")
    core, rim = spread_out(span_start, span_len, weighted, teach_dev)
    return (student_out, add_rim(core, rim, near, far))


def solution(mesh):
    return jax.shard_map(
        body,
        mesh=mesh,
        in_specs=(
            P("ctx", "tp"),
            P("ctx", "tp"),
            P(None, "ctx", None),
            P(None, "tp"),
            P("ctx", "tp"),
            P("ctx"),
            P("ctx"),
        ),
        out_specs=(P("ctx", "tp"), P("ctx", "tp")),
        check_vma=False,
    )
```

```python
import functools
import math

import jax
import jax.numpy as jnp
from jax import lax
from jax.experimental import pallas as pl
from jax.experimental.pallas import tpu as pltpu
from jax.sharding import PartitionSpec as P


HEADS = 32
KVH = 4
HD = 128
HALO = 8
GROUP = 4

F32 = jnp.float32
BF16 = jnp.bfloat16
floor_score = -1e30
exp2_scale = math.log2(math.e) / math.sqrt(HD)

ATTN_VMEM = 9 * 1024 * 1024
PROJECT_VMEM = 10 * 1024 * 1024
FINISH_VMEM = 10 * 1024 * 1024


def odd_swapped(value, axis):
    count = lax.axis_size(axis)
    return lax.ppermute(
        value, axis, [(i, i + 1 if i % 2 else i - 1) for i in range(1, count - 1)]
    )


def swapped(value, axis, bit):
    count = lax.axis_size(axis)
    return lax.ppermute(value, axis, [(source, source ^ bit) for source in range(count)])


def attention_step(
    query_ref, heads, keys, values, state, hidden, diagonal, peak_ref, accum_ref
):
    rows = keys[0].shape[0]
    ones = jnp.ones((rows, HD), BF16)
    padded = [jnp.concatenate([block, ones], axis=1) for block in values]

    def product(head):
        query = query_ref[:, head * HD : (head + 1) * HD]
        return [
            lax.dot_general(query, block, (((1,), (1,)), ((), ())), preferred_element_type=F32)
            for block in keys
        ]

    scores = product(0)
    for head in range(heads):
        following = product(head + 1) if head + 1 < heads else None
        if diagonal is not None:
            scores[0] = jnp.where(diagonal, scores[0], floor_score)
        if hidden is None:
            top = functools.reduce(jnp.maximum, scores)
            top = jnp.max(top, axis=1, keepdims=True) * exp2_scale
        else:
            tops = [
                jnp.max(block, axis=1, keepdims=True) * exp2_scale - off
                for block, off in zip(scores, hidden)
            ]
            top = functools.reduce(jnp.maximum, tops)
        peak = top if state is None else jnp.maximum(state[head][0], top)
        accum = None if state is None else state[head][1][...] * jnp.exp2(state[head][0] - peak)
        for index, (block, value) in enumerate(zip(scores, padded)):
            shift = peak if hidden is None else peak + hidden[index]
            weights = jnp.exp2(block * exp2_scale - shift).astype(BF16)
            added = jnp.dot(weights, value, preferred_element_type=F32)
            accum = added if accum is None else accum + added
        peak_ref[:, head : head + 1] = peak
        accum_ref[head] = accum
        scores = following


def own_kernel(heads, query_ref, own_ref, side_ref, other_ref, peak_ref, accum_ref):
    rows = query_ref.shape[0]
    place = lax.rem(lax.axis_index("ctx"), GROUP)
    pieces = [own_ref, side_ref, other_ref.at[0], other_ref.at[1]]
    hidden = [0.0] + [
        jnp.where((place ^ flip) < place, 0.0, -floor_score).astype(F32) for flip in (2, 1, 3)
    ]
    diagonal = lax.broadcasted_iota(jnp.int32, (rows, rows), 1) <= lax.broadcasted_iota(
        jnp.int32, (rows, rows), 0
    )
    attention_step(
        query_ref,
        heads,
        [p[0] for p in pieces],
        [p[1] for p in pieces],
        None,
        hidden,
        diagonal,
        peak_ref,
        accum_ref,
    )


def weight_rows(step, start, depth, lane_rows, tp_count):
    lane = lax.rem(lax.axis_index("tp") + tp_count - step, tp_count)
    return pl.ds(pl.multiple_of(lane * lane_rows + start, HD), depth)


def fetches(blocks, lanes, weight_hbm, refs, sems):
    return [
        pltpu.make_async_copy(weight_hbm.at[weight_rows(*block, *lanes), :], ref, sems.at[index])
        for index, (block, ref) in enumerate(zip(blocks, refs))
    ]


def more_kernel(heads, first, turns, fetch, lanes, query_ref, *refs):
    parts = [(stages, refs[4 * k : 4 * k + 4]) for k, stages in enumerate(turns)]
    refs = refs[4 * len(turns) :]
    (peak_in, accum_in, weight_hbm, out_ref), refs = refs[:4], refs[4:]
    peak_ref, accum_ref, sems = refs[-3:]
    copies = fetches(fetch, lanes, weight_hbm, refs[:-3], sems)
    for copy in copies:
        copy.start()
    for head in range(heads):
        accum_ref[head] = accum_in[first + head]
        peak_ref[:, head : head + 1] = peak_in[:, first + head : first + head + 1]
    group = lax.div(lax.axis_index("ctx"), GROUP)
    for stages, blocks in parts:

        def step(index, carry, stages=stages, blocks=blocks):
            @pl.when((group ^ (index + stages[0])) < group)
            def _():
                pieces = [ref.at[index] for ref in blocks]
                state = [
                    (peak_ref[:, head : head + 1], accum_ref.at[head]) for head in range(heads)
                ]
                attention_step(
                    query_ref,
                    heads,
                    [p[0] for p in pieces],
                    [p[1] for p in pieces],
                    state,
                    None,
                    None,
                    peak_ref,
                    accum_ref,
                )

            return carry

        lax.fori_loop(0, len(stages), step, 0)
    for head in range(heads):
        accum = accum_ref[head]
        out_ref[:, head * HD : (head + 1) * HD] = (accum[:, :HD] / accum[:, HD:]).astype(BF16)
    for copy in copies:
        copy.wait()


VMEM_SPEC = pl.BlockSpec(memory_space=pltpu.VMEM)
HBM_SPEC = pl.BlockSpec(memory_space=pltpu.HBM)
MIB = 1024 * 1024


def attention_cost(rows, heads, keys):
    return pl.CostEstimate(
        flops=4 * rows * heads * keys * HD * 2,
        transcendentals=rows * heads * keys,
        bytes_accessed=2 * MIB,
    )


def state_shapes(rows, heads):
    return [((rows, HD), F32), ((heads, rows, 2 * HD), F32)]


def query_spec(rows, heads, kv):
    return pl.BlockSpec((rows, heads * HD), lambda i: (0, kv))


def attend_own(queries, kv, heads, own, side, other):
    rows = queries.shape[0]
    return pl.pallas_call(
        functools.partial(own_kernel, heads),
        grid=(1,),
        in_specs=[query_spec(rows, heads, kv)] + [VMEM_SPEC] * 3,
        out_specs=[VMEM_SPEC] * 2,
        out_shape=[jax.ShapeDtypeStruct(*shape) for shape in state_shapes(rows, heads)],
        compiler_params=pltpu.CompilerParams(vmem_limit_bytes=ATTN_VMEM),
        cost_estimate=attention_cost(rows, heads, GROUP * rows),
        name="attend_own",
    )(queries, own, side, other)


def fetched(fetch, out_weight):
    return [pltpu.VMEM((depth, out_weight.shape[1]), BF16) for _, _, depth in fetch]


def attend_more(
    queries, kv, per_own, first, heads, turns, blocks, state, fetch, lanes, out_weight
):
    rows = queries.shape[0]
    return pl.pallas_call(
        functools.partial(more_kernel, heads, first, turns, fetch, lanes),
        grid=(1,),
        in_specs=[query_spec(rows, heads, (kv * per_own + first) // heads)]
        + [VMEM_SPEC] * (len(blocks) + 2)
        + [HBM_SPEC],
        out_specs=[VMEM_SPEC] * (1 + len(fetch)),
        out_shape=[jax.ShapeDtypeStruct((rows, heads * HD), BF16)] + fetched(fetch, out_weight),
        scratch_shapes=[pltpu.VMEM(*shape) for shape in state_shapes(rows, heads)]
        + [pltpu.SemaphoreType.DMA((max(1, len(fetch)),))],
        compiler_params=pltpu.CompilerParams(vmem_limit_bytes=ATTN_VMEM),
        cost_estimate=attention_cost(rows, heads, GROUP * len(sum(turns, [])) * rows),
        name="attend_more",
    )(queries, *blocks, *state, out_weight)


def upright(row):
    count = row.shape[1]
    same = iota((count, count), 0) == iota((count, count), 1)
    return jnp.sum(jnp.where(same, row, 0), axis=1, keepdims=True)


def member_of(starts, lens, columns):
    return ((columns >= starts) & (columns < starts + lens)).astype(F32).astype(BF16)


def iota(shape, axis):
    return lax.broadcasted_iota(jnp.int32, shape, axis)


def is_odd():
    return lax.rem(lax.axis_index("ctx"), 2) == 1


def rim_rows(index, teach):
    below = (index < HALO) == is_odd()
    index = jnp.where(index < HALO, index, index - HALO)
    return jnp.where(below, index - HALO, index + teach)


def joined(pieces, piece_refs):
    runs = []
    for (block, start, depth), ref in zip(pieces, piece_refs):
        if runs and runs[-1][0] == block and runs[-1][1] + runs[-1][2] == start:
            runs[-1][2] += depth
            runs[-1][3].append(ref)
        else:
            runs.append([block, start, depth, [ref]])
    return [
        (block, start, depth, jnp.concatenate([ref[...] for ref in refs], axis=1))
        for block, start, depth, refs in runs
    ]


def product(runs, weight_refs, span, total):
    for block, start, depth, value in runs:
        rows = weight_refs[block][start : start + depth, span]
        total += jnp.dot(value, rows, preferred_element_type=F32)
    return total


def base_kernel(pieces, cols, start_ref, len_ref, *refs):
    student_ref, teacher_ref, near_ref, far_ref = refs[:4]
    piece_refs, weight_refs = refs[4 : 4 + len(pieces)], refs[4 + len(pieces) : -2]
    base_ref, target_ref = refs[-2:]
    rows, width = student_ref.shape
    teach = teacher_ref.shape[0]
    starts = upright(start_ref[...]) - lax.axis_index("ctx") * teach
    lens = upright(len_ref[...])
    inner = member_of(starts, lens, iota((rows, teach), 1))
    outer = member_of(starts, lens, rim_rows(iota((rows, 2 * HALO), 1), teach))
    share = 1.0 / lens.astype(F32)
    runs = joined(pieces, piece_refs)
    for step in range(width // cols):
        span = slice(step * cols, (step + 1) * cols)
        target = jnp.dot(inner, teacher_ref[:, span], preferred_element_type=F32)
        halo = [ref[:, span].astype(F32) for ref in (near_ref, far_ref)]
        halo = jnp.concatenate(halo, axis=0).astype(BF16)
        target += jnp.dot(outer, halo, preferred_element_type=F32)
        target_ref[:, span] = target * share
        total = student_ref[:, span].astype(F32)
        base_ref[:, span] = product(runs, weight_refs, span, total)


def late_kernel(pieces, count, fetch, lanes, cols, base_ref, *refs):
    piece_refs, weight_refs = refs[: len(pieces)], refs[len(pieces) : len(pieces) + count]
    weight_hbm, out_ref, last_ref, sems = refs[len(pieces) + count :]
    copies = fetches(fetch, lanes, weight_hbm, [last_ref], sems)
    for copy in copies:
        copy.start()
    runs = joined(pieces, piece_refs)
    for start in range(0, base_ref.shape[1], cols):
        span = slice(start, start + cols)
        out_ref[:, span] = product(runs, weight_refs, span, base_ref[:, span])
    for copy in copies:
        copy.wait()


def product_cost(rows, width, pieces):
    depth = sum(piece[2] for piece in pieces)
    return pl.CostEstimate(
        flops=2 * rows * width * depth,
        transcendentals=0,
        bytes_accessed=2 * depth * width + 10 * rows * width,
    )


def project_base(pieces, values, weights, starts, lens, student, teacher, halos):
    rows, width = student.shape
    return pl.pallas_call(
        functools.partial(base_kernel, pieces, min(1024, width)),
        in_specs=[VMEM_SPEC] * (6 + len(values) + len(weights)),
        out_specs=[VMEM_SPEC] * 2,
        out_shape=[jax.ShapeDtypeStruct((rows, width), F32)] * 2,
        compiler_params=pltpu.CompilerParams(vmem_limit_bytes=PROJECT_VMEM),
        cost_estimate=product_cost(rows, width, pieces),
        name="project_base",
    )(starts[None, :], lens[None, :], student, teacher, *halos, *values, *weights)


def project_late(pieces, values, weights, base, fetch, lanes, out_weight):
    rows, width = base.shape
    return pl.pallas_call(
        functools.partial(late_kernel, pieces, len(weights), fetch, lanes, min(1024, width)),
        in_specs=[VMEM_SPEC] * (1 + len(values) + len(weights)) + [HBM_SPEC],
        out_specs=[VMEM_SPEC] * 2,
        out_shape=[jax.ShapeDtypeStruct((rows, width), F32)] + fetched(fetch, out_weight),
        scratch_shapes=[pltpu.SemaphoreType.DMA((1,))],
        compiler_params=pltpu.CompilerParams(vmem_limit_bytes=PROJECT_VMEM),
        cost_estimate=product_cost(rows, width, pieces),
        name="project_late",
    )(base, *values, *weights, out_weight)


def final_kernel(count, cols, teach, start_ref, len_ref, base_ref, target_ref, *refs):
    piece_refs, weight_ref = refs[:count], refs[count]
    student_out, weighted_ref, near_ref, far_ref, student_buf, sems = refs[count + 1 :]
    rows, width = base_ref.shape
    starts, lens = start_ref[...] - lax.axis_index("ctx") * teach, len_ref[...]
    outer_t = member_of(starts, lens, rim_rows(iota((2 * HALO, rows), 0), teach))
    share = 1.0 / upright(lens).astype(F32)
    value = jnp.concatenate([ref[...] for ref in piece_refs], axis=1)
    copies = []
    for index, start in enumerate(range(0, width, cols)):
        span = slice(start, start + cols)
        total = base_ref[:, span]
        total += jnp.dot(value, weight_ref[:, span], preferred_element_type=F32)
        student_buf[:, span] = total.astype(BF16)
        copy = pltpu.make_async_copy(
            student_buf.at[:, span], student_out.at[:, span], sems.at[index]
        )
        copy.start()
        copies.append(copy)
        weighted = ((total - target_ref[:, span]) * share).astype(BF16)
        weighted_ref[:, span] = weighted
        edge = jnp.dot(outer_t, weighted, preferred_element_type=F32)
        near_ref[:, span] = edge[:HALO].astype(BF16)
        far_ref[:, span] = edge[HALO:].astype(BF16)
    for copy in copies:
        copy.wait()


def finish(starts, lens, base, target, teach, pieces, weight):
    rows, width = base.shape
    count, depth = len(pieces), weight.shape[0]
    cols = min(1024, width)
    return pl.pallas_call(
        functools.partial(final_kernel, count, cols, teach),
        in_specs=[VMEM_SPEC] * (5 + count),
        out_specs=[HBM_SPEC] + [VMEM_SPEC] * 3,
        scratch_shapes=[pltpu.VMEM((rows, width), BF16), pltpu.SemaphoreType.DMA((width // cols,))],
        out_shape=[
            jax.ShapeDtypeStruct((rows, width), BF16),
            jax.ShapeDtypeStruct((rows, width), BF16),
            jax.ShapeDtypeStruct((HALO, width), BF16),
            jax.ShapeDtypeStruct((HALO, width), BF16),
        ],
        compiler_params=pltpu.CompilerParams(vmem_limit_bytes=FINISH_VMEM),
        cost_estimate=pl.CostEstimate(
            flops=2 * rows * width * depth,
            transcendentals=0,
            bytes_accessed=2 * depth * width + 10 * rows * width,
        ),
        name="finish",
    )(starts[None, :], lens[None, :], base, target, *pieces, weight)


def spread_kernel(cols, start_ref, len_ref, weighted_ref, core_out, rim_ref, core_buf, sems):
    rows, width = weighted_ref.shape
    teach = core_buf.shape[0]
    starts, lens = start_ref[...] - lax.axis_index("ctx") * teach, len_ref[...]
    inner_t = member_of(starts, lens, iota((teach, rows), 0))
    copies = []
    for index, start in enumerate(range(0, width, cols)):
        span = slice(start, start + cols)
        core = jnp.dot(inner_t, weighted_ref[:, span], preferred_element_type=F32)
        core_buf[:, span] = core.astype(BF16)
        rim_ref[: 2 * HALO, span] = core[: 2 * HALO]
        rim_ref[2 * HALO :, span] = core[teach - 2 * HALO :]
        copy = pltpu.make_async_copy(
            core_buf.at[:, span], core_out.at[:, span], sems.at[index]
        )
        copy.start()
        copies.append(copy)
    for copy in copies:
        copy.wait()


def spread_out(starts, lens, weighted, teach):
    rows, width = weighted.shape
    cols = min(1024, width)
    return pl.pallas_call(
        functools.partial(spread_kernel, cols),
        in_specs=[VMEM_SPEC] * 3,
        out_specs=[HBM_SPEC, VMEM_SPEC],
        scratch_shapes=[pltpu.VMEM((teach, width), BF16), pltpu.SemaphoreType.DMA((width // cols,))],
        out_shape=[
            jax.ShapeDtypeStruct((teach, width), BF16),
            jax.ShapeDtypeStruct((4 * HALO, width), F32),
        ],
        compiler_params=pltpu.CompilerParams(vmem_limit_bytes=FINISH_VMEM),
        cost_estimate=pl.CostEstimate(
            flops=2 * rows * width * teach, transcendentals=0, bytes_accessed=2 * teach * width
        ),
        name="spread_out",
    )(starts[None, :], lens[None, :], weighted)


def rim_kernel(core_in, rim_ref, near_ref, far_ref, core_out, block_ref, sems):
    del core_in
    near, far = near_ref[...].astype(F32), far_ref[...].astype(F32)
    rest = jnp.zeros_like(near)
    odd = is_odd()
    first = jnp.concatenate([jnp.where(odd, near, far), rest], axis=0)
    last = jnp.concatenate([rest, jnp.where(odd, far, near)], axis=0)
    height = 2 * HALO
    copies = []
    for slot, (part, row) in enumerate(((first, 0), (last, core_out.shape[0] - height))):
        block_ref[slot] = (rim_ref[slot * height : (slot + 1) * height] + part).astype(BF16)
        copy = pltpu.make_async_copy(
            block_ref.at[slot], core_out.at[pl.ds(row, height), :], sems.at[slot]
        )
        copy.start()
        copies.append(copy)
    for copy in copies:
        copy.wait()


def add_rim(core, rim, near, far):
    width = core.shape[1]
    return pl.pallas_call(
        rim_kernel,
        in_specs=[HBM_SPEC] + [VMEM_SPEC] * 3,
        out_specs=HBM_SPEC,
        out_shape=jax.ShapeDtypeStruct(core.shape, core.dtype),
        scratch_shapes=[pltpu.VMEM((2, 2 * HALO, width), BF16), pltpu.SemaphoreType.DMA((2,))],
        input_output_aliases={0: 0},
        compiler_params=pltpu.CompilerParams(vmem_limit_bytes=4 * MIB),
        name="add_rim",
    )(core, rim, near, far)


def body(student_rows, queries, keys_values, out_weight, teacher_rows, span_start, span_len):
    ctx_count = lax.axis_size("ctx")
    tp_lane = lax.axis_index("tp")
    tp_count = lax.axis_size("tp")
    teach_dev = teacher_rows.shape[0]
    heads_dev = queries.shape[1] // HD
    group_size = HEADS // KVH
    kv_dev = max(1, heads_dev // group_size)
    per_own = heads_dev // kv_dev
    groups = ctx_count // GROUP
    kv_first = tp_lane * heads_dev // group_size

    owns = [
        lax.dynamic_slice_in_dim(keys_values, (kv_first + kv) * HD, HD, 2) for kv in range(kv_dev)
    ]
    place = jnp.where(is_odd(), 0, teach_dev - HALO)
    edges = [
        lax.dynamic_slice_in_dim(teacher_rows, start, HALO, 0)
        for start in (place, teach_dev - HALO - place)
    ]
    halos = [swapped(edges[0], "ctx", 1)]
    halos.append(odd_swapped(edges[1], "ctx"))
    both = jnp.stack(owns)
    side_all = swapped(both, "ctx", 2)
    other_all = swapped(jnp.stack([both, side_all], axis=1), "ctx", 1)
    stages = list(range(1, groups))
    lanes = (heads_dev * HD, tp_count)
    depth = per_own * HD
    weights = {}
    out_weight = pltpu.with_memory_space_constraint(out_weight, pltpu.HBM)
    attended = []
    for kv in range(kv_dev):
        lifts = []
        for step in range(1, groups):
            lifts.append(swapped(owns[kv], "ctx", GROUP * step))
        state = attend_own(queries, kv, per_own, owns[kv], side_all[kv], other_all[kv])
        turns = [stages] if kv or len(stages) < 2 else [stages[:1], stages[1:]]
        blocks = []
        for turn, chosen in enumerate(turns):
            straight = jnp.stack([lifts[step - 1] for step in chosen])
            crossed = swapped(straight, "ctx", 2)
            if turn < len(turns) - 1:
                pair = swapped(jnp.concatenate([straight, crossed]), "ctx", 1)
                blocks += [straight, crossed, pair[: len(chosen)], pair[len(chosen) :]]
                continue
            blocks += [straight, crossed, swapped(straight, "ctx", 1)]
            blocks.append(swapped(crossed, "ctx", 1))
        final = kv == kv_dev - 1
        parts = 2 if final and per_own % 2 == 0 else 1
        heads = per_own // parts
        for part in range(parts):
            first = part * heads
            if not final:
                wanted = [(0, kv)]
            else:
                wanted = [(0, kv)] + [
                    (step, other)
                    for step in range(1, tp_count)
                    for other in range(kv_dev)
                    if (step, other) != (tp_count - 1, kv)
                ]
                share = -(-len(wanted) // parts)
                wanted = wanted[part * share : (part + 1) * share]
            fetch = [(step, other * depth, depth) for step, other in wanted]
            result = attend_more(
                queries, kv, per_own, first, heads, turns, blocks, state, fetch, lanes, out_weight
            )
            weights.update(zip(wanted, result[1:]))
            attended.append((kv, part, first * HD, result[0]))

    early, late, rest = [], [], []
    for kv, part, start, value in attended:
        (late if kv == kv_dev - 1 else early).append(((0, kv), start, value))
    for step in range(1, tp_count):
        ring = [(i, (i + step) % tp_count) for i in range(tp_count)]
        for kv, part, start, value in attended:
            got = lax.ppermute(value, "tp", ring)
            if kv == kv_dev - 1 and step == tp_count - 1:
                rest.append(got)
            else:
                late.append(((step, kv), start, got))

    def products(entries):
        blocks = list(dict.fromkeys(block for block, _, _ in entries))
        pieces = [(blocks.index(block), at, value.shape[1]) for block, at, value in entries]
        return pieces, [value for _, _, value in entries], [weights[block] for block in blocks]

    base, target = project_base(
        *products(early), span_start, span_len, student_rows, teacher_rows, halos
    )
    fetch = [(tp_count - 1, (kv_dev - 1) * depth, depth)]
    base, weight = project_late(*products(late), base, fetch, lanes, out_weight)
    student_out, weighted, near, far = finish(
        span_start, span_len, base, target, teach_dev, rest, weight
    )
    near = swapped(near, "ctx", 1)
    far = odd_swapped(far, "ctx")
    core, rim = spread_out(span_start, span_len, weighted, teach_dev)
    return (student_out, add_rim(core, rim, near, far))


def solution(mesh):
    return jax.shard_map(
        body,
        mesh=mesh,
        in_specs=(
            P("ctx", "tp"),
            P("ctx", "tp"),
            P(None, "ctx", None),
            P(None, "tp"),
            P("ctx", "tp"),
            P("ctx"),
            P("ctx"),
        ),
        out_specs=(P("ctx", "tp"), P("ctx", "tp")),
        check_vma=False,
    )
```
